32 devices in a mesh: groups: 2 (over y), seq: 4 (over z), head: 2 (over x), sub: 2 (over core).
Axes of the slice: x: 2, y: 2, z: 4, core: 2. Of those that a mesh axis runs over, the one named last changes fastest.
Arguments:
- queries: bfloat16 [128, 128, 16, 128], P(('groups', 'seq'), None, ('head', 'sub')), parts along dimension 0, may hold values from -6 to 6
- keys: bfloat16 [128, 128, 16, 128], P(('groups', 'seq'), None, ('head', 'sub')), parts along dimension 0, may hold values from -6 to 6
- values: bfloat16 [128, 128, 16, 2, 128], P(('groups', 'seq'), None, ('head', 'sub')), parts along dimension 0, may hold values from -6 to 6
- log_decay: bfloat16 [128, 128, 16, 2], P(('groups', 'seq'), None, ('head', 'sub')), parts along dimension 0, may hold values from -0.8 to 0
- write_rate: bfloat16 [128, 128, 16, 2], P(('groups', 'seq'), None, ('head', 'sub')), parts along dimension 0, may hold values from 0.049804688 to 0.94921875
- norm_gain: bfloat16 [128], replicated, may hold values from 0.25 to 1.75
- parent_cache: float32 [32, 16, 2, 128, 128], P(('groups', 'seq'), ('head', 'sub')), parts along dimension 0, may hold values from -3 to 3
- order: int32 [128], P('groups'), parts along dimension 0, may hold values from 0 to 63, as said below
- parent_owner: int32 [128], P('groups'), parts along dimension 0, may hold values from 0 to 3, as said below
- parent_slot: int32 [128], P('groups'), parts along dimension 0, may hold values from 0 to 3
- token_count: int32 [128], P('groups'), parts along dimension 0, may hold values from 64 to 128, as said below
Outputs:
- mixed: bfloat16 [128, 128, 16, 2, 128], P(('groups', 'seq'), None, ('head', 'sub')), parts along dimension 0
- final_state: float32 [128, 16, 2, 128, 128], P(('groups', 'seq'), ('head', 'sub')), parts along dimension 0
The draws below stay inside these ranges and needn't reach their ends.
There are 2 independent parts, one for each index of `groups`. The reference program is written for one: setup_inputs(seed, part) draws one part's arguments, and reference() takes and returns one part's arrays. A program takes and returns all parts, laid end to end along the dimension named above; an argument that names none is the same for every part. Nothing has to cross between parts.
Inputs may be any that keep to these rules, and one draw needn't show every extreme that they name: A permutation; slot j = p * 16 + s * 4 + r with r < 4 is processed by seq device p and holds an expansion that arrives on seq device s, so order[j] // 16 = s. `parent_owner`: among the 16 expansions processed by one seq device at most 8 have their parent on one owner, and on some device exactly 8 do. `token_count`: multiples of 64; some expansion has 128 and some has 64.
All inputs are finite; a program needn't handle non-finite values.
Results may differ from the reference program's by a relative error of at most 0.001.
Values may be sent and summed in bfloat16 or wider, within the bound.
A program may use at most 192 MiB of HBM per device.

```python
import jax
import jax.numpy as jnp
from jax import lax

KEY_HEAD_COUNT = 16
DK = 128
DV = 128
TOKEN_SLOTS = 128
SPAN = 64
EXP_DEV = 16
PAR_DEV = 4
GROUP_EXPANSIONS = 64
PARENTS = 16
CAP = 8
N_SEQ = 4


def owner_plan(key):
    key_perm, key_base, key_pair, key_force, key_shuffle = jax.random.split(jax.random.fold_in(key, 11), 5)
    per_peer = EXP_DEV // N_SEQ
    arrivals = jax.vmap(lambda single: jax.random.permutation(single, EXP_DEV))(jax.random.split(key_perm, N_SEQ))
    slot_grid = arrivals.reshape(N_SEQ, N_SEQ, per_peer) + (jnp.arange(N_SEQ, dtype=jnp.int32) * EXP_DEV)[:, None, None]
    order_ids = jnp.transpose(slot_grid, (1, 0, 2)).reshape(-1).astype(jnp.int32)
    base_owner = jax.random.randint(key_base, (N_SEQ,), 0, N_SEQ)
    paired = jax.random.randint(key_pair, (N_SEQ,), 0, 2)
    forced = jax.random.randint(key_force, (), 0, N_SEQ)
    paired = jnp.where(jnp.arange(N_SEQ) == forced, 1, paired)
    shuffled = jax.vmap(lambda single: jax.random.permutation(single, EXP_DEV))(jax.random.split(key_shuffle, N_SEQ))
    offsets = jnp.where(paired[:, None] == 1, shuffled // CAP, shuffled)
    owner_by_slot = ((base_owner[:, None] + offsets) % N_SEQ).reshape(-1).astype(jnp.int32)
    owners = jnp.zeros((GROUP_EXPANSIONS,), jnp.int32).at[order_ids].set(owner_by_slot)
    return (order_ids, owners)


def draw_order(key, part):
    return owner_plan(key)[0]


def draw_parent_owner(key, part):
    return owner_plan(key)[1]


def draw_token_count(key, part):
    key_blocks, key_top, key_low = jax.random.split(jax.random.fold_in(key, 23), 3)
    top_blocks = TOKEN_SLOTS // SPAN
    blocks = jax.random.randint(key_blocks, (GROUP_EXPANSIONS,), 1, top_blocks + 1)
    longest = jax.random.randint(key_top, (), 0, GROUP_EXPANSIONS)
    shortest = (longest + 1 + jax.random.randint(key_low, (), 0, GROUP_EXPANSIONS - 1)) % GROUP_EXPANSIONS
    positions = jnp.arange(GROUP_EXPANSIONS)
    blocks = jnp.where(positions == longest, top_blocks, blocks)
    blocks = jnp.where(positions == shortest, 1, blocks)
    return (blocks * SPAN).astype(jnp.int32)


def draw_log_decay(key, part):
    every_key_row = jax.random.split(jax.random.fold_in(key, 37), 7)
    fast_share = 0.5
    fast_heads = jax.random.uniform(every_key_row[0], (KEY_HEAD_COUNT, 2)) < fast_share
    fast_rate = jnp.exp(jax.random.uniform(every_key_row[1], (KEY_HEAD_COUNT, 2), jnp.float32, jnp.log(1.0 / 50.0), jnp.log(1.0 / 30.0)))
    slow_rate = jnp.exp(jax.random.uniform(every_key_row[2], (KEY_HEAD_COUNT, 2), jnp.float32, jnp.log(3e-05), jnp.log(0.0006)))
    per_head_rate = jnp.where(fast_heads, fast_rate, slow_rate)
    growth_multiplier = jnp.exp(jax.random.uniform(every_key_row[3], (GROUP_EXPANSIONS, 1, 1, 1), jnp.float32, jnp.log(0.5), jnp.log(2.0)))
    jaggedness = jax.random.uniform(every_key_row[4], (GROUP_EXPANSIONS, TOKEN_SLOTS, KEY_HEAD_COUNT, 2), jnp.float32, 0.5, 1.5)
    flurries = jax.random.uniform(every_key_row[5], (GROUP_EXPANSIONS, TOKEN_SLOTS, KEY_HEAD_COUNT, 2)) < 2.0 / TOKEN_SLOTS
    flurry_depth = jnp.log(jax.random.uniform(every_key_row[6], (GROUP_EXPANSIONS, TOKEN_SLOTS, KEY_HEAD_COUNT, 2), jnp.float32, 0.5, 0.8))
    return (-(per_head_rate * growth_multiplier * jaggedness) + jnp.where(flurries, flurry_depth, 0.0)).astype(jnp.bfloat16)


def touch_ends(drawn, key, smallest, high):
    shape = drawn.shape
    spot = [jax.random.randint(jax.random.fold_in(key, axis), (), 0, shape[axis]) for axis in range(len(shape))]
    drawn = drawn.at[tuple(spot)].set(smallest)
    longest = shape.index(max(shape))
    spot[longest] = (spot[longest] + 1) % shape[longest]
    return drawn.at[tuple(spot)].set(high)


def levels(rng, extent, cuts, smallest, high):
    gain, own = 1.0, jax.random.fold_in(rng, 6)
    for axis_at, parts in cuts:
        heights = jnp.exp(jax.random.uniform(jax.random.fold_in(own, axis_at), (parts,), jnp.float32, smallest / len(cuts), high / len(cuts)))
        gain = gain * jnp.repeat(heights, extent[axis_at] // parts).reshape([-1 if axis == axis_at else 1 for axis in range(len(extent))])
    return gain


def scatter_about(own_key, shape, width, bound, cuts=(), kind=jnp.bfloat16):
    values = width * jax.random.normal(own_key, shape, jnp.float32)
    if cuts:
        values = values * levels(own_key, shape, cuts, -0.22, 0.18)
    return jnp.clip(values, -bound, bound).astype(kind)


def setup_inputs(seed: int = 0, part: int = 0) -> dict:
    arg_keys = jax.random.split(jax.random.key(seed), 12)
    part_keys = jax.random.split(jax.random.fold_in(arg_keys[11], part), 12)
    queries = scatter_about(part_keys[0], (GROUP_EXPANSIONS, TOKEN_SLOTS, KEY_HEAD_COUNT, DK), 1.0, 6.0, ((0, 4), (2, 4)))
    keys = scatter_about(part_keys[1], (GROUP_EXPANSIONS, TOKEN_SLOTS, KEY_HEAD_COUNT, DK), 1.0, 6.0, ((0, 4), (2, 4)))
    values = scatter_about(part_keys[2], (GROUP_EXPANSIONS, TOKEN_SLOTS, KEY_HEAD_COUNT, 2, DV), 1.0, 6.0, ((0, 4), (2, 4)))
    log_decay = draw_log_decay(jax.random.fold_in(jax.random.fold_in(arg_keys[11], part), 71), part)
    write_rate = jnp.clip(0.049804688 + 0.89941406 * jax.random.uniform(part_keys[4], (GROUP_EXPANSIONS, TOKEN_SLOTS, KEY_HEAD_COUNT, 2), jnp.float32) ** levels(part_keys[4], (GROUP_EXPANSIONS, TOKEN_SLOTS, KEY_HEAD_COUNT, 2), ((0, 4), (2, 4)), -0.2, 0.2), 0.049804688, 0.94921875).astype(jnp.bfloat16)
    norm_gain = jnp.clip(1.0 + 0.15 * jax.random.normal(arg_keys[5], (DV,), jnp.float32), 0.25, 1.75).astype(jnp.bfloat16)
    parent_cache = scatter_about(part_keys[6], (PARENTS, KEY_HEAD_COUNT, 2, DK, DV), 0.5, 3.0, ((0, 4), (1, 4)), jnp.float32)
    order = draw_order(jax.random.fold_in(jax.random.fold_in(arg_keys[11], part), 71), part)
    parent_owner = draw_parent_owner(jax.random.fold_in(jax.random.fold_in(arg_keys[11], part), 71), part)
    parent_slot = touch_ends(jax.random.randint(part_keys[9], (GROUP_EXPANSIONS,), 0, PAR_DEV), jax.random.fold_in(part_keys[9], 1), 0, PAR_DEV - 1).astype(jnp.int32)
    token_count = draw_token_count(jax.random.fold_in(jax.random.fold_in(arg_keys[11], part), 71), part)
    return {"queries": queries, "keys": keys, "values": values, "log_decay": log_decay, "write_rate": write_rate, "norm_gain": norm_gain, "parent_cache": parent_cache, "order": order, "parent_owner": parent_owner, "parent_slot": parent_slot, "token_count": token_count}


exact_mode = lax.Precision.HIGHEST
norm_epsilon = 1e-06

def inverse_unit(lower_part):
    block_len = lower_part.shape[-1]
    identity = jnp.eye(block_len, dtype=jnp.float32)
    result = identity - lower_part
    powered = lower_part
    for repeat_no in range(block_len.bit_length() - 2):
        powered = jnp.einsum('...ij,...jk->...ik', powered, powered, precision=exact_mode)
        result = result + jnp.einsum('...ij,...jk->...ik', result, powered, precision=exact_mode)
    return result

def arrange(queries, keys, values, log_decay, write_rate, token_count, block_len):
    expansions, length, key_heads, key_dim = queries.shape
    value_dim = values.shape[-1]
    block_count = length // block_len
    head_rows = expansions * key_heads * 2
    positions = lax.broadcasted_iota(jnp.int32, (expansions, length), 1)
    live_mask = positions < token_count[:, None]
    keys_unit = keys.astype(jnp.float32)
    keys_unit = keys_unit / jnp.sqrt(lax.optimization_barrier(jnp.sum(keys_unit * keys_unit, axis=-1, keepdims=True)) + norm_epsilon)

    def spread_heads(tensor):
        turned = jnp.transpose(tensor, (0, 2, 1, 3))[:, :, None]
        widened = jnp.broadcast_to(turned, (expansions, key_heads, 2, length, key_dim))
        return widened.reshape(head_rows, block_count, block_len, key_dim)
    query_rows = spread_heads(queries.astype(jnp.float32))
    key_rows = spread_heads(keys_unit)
    value_rows = jnp.transpose(values.astype(jnp.float32), (0, 2, 3, 1, 4)).reshape(head_rows, block_count, block_len, value_dim)
    live_wide = live_mask[:, :, None, None]
    decay_rows = jnp.transpose(jnp.where(live_wide, log_decay.astype(jnp.float32), 0.0), (0, 2, 3, 1)).reshape(head_rows, block_count, block_len)
    rate_rows = jnp.transpose(jnp.where(live_wide, write_rate.astype(jnp.float32), 0.0), (0, 2, 3, 1)).reshape(head_rows, block_count, block_len)
    live_rows = jnp.broadcast_to(live_mask[:, None, None, :], (expansions, key_heads, 2, length)).reshape(head_rows, length)
    return (query_rows, key_rows, value_rows, decay_rows, rate_rows, live_rows)

def within_spans(query_rows, key_rows, value_rows, decay_rows, rate_rows):
    block_len = decay_rows.shape[-1]
    cumulative = jnp.cumsum(decay_rows, axis=-1)
    spread_log = cumulative[..., :, None] - cumulative[..., None, :]
    row_ids = lax.broadcasted_iota(jnp.int32, (block_len, block_len), 0)
    col_ids = lax.broadcasted_iota(jnp.int32, (block_len, block_len), 1)
    inclusive = row_ids >= col_ids
    strict = row_ids > col_ids
    decay_pair = jnp.where(inclusive, jnp.exp(jnp.where(inclusive, spread_log, 0.0)), 0.0)
    key_key = jnp.einsum('bncd,bnjd->bncj', key_rows, key_rows, precision=exact_mode)
    lower_part = jnp.where(strict, rate_rows[..., :, None] * key_key * decay_pair, 0.0)
    inverse = inverse_unit(lower_part)
    scaled_keys = key_rows * (rate_rows * jnp.exp(cumulative))[..., None]
    scaled_values = value_rows * rate_rows[..., None]
    weights_w = jnp.einsum('bncj,bnjd->bncd', inverse, scaled_keys, precision=exact_mode)
    updates_u = jnp.einsum('bncj,bnjd->bncd', inverse, scaled_values, precision=exact_mode)
    query_key = jnp.einsum('bncd,bnjd->bncj', query_rows, key_rows, precision=exact_mode)
    local_mix = query_key * decay_pair
    decayed_queries = query_rows * jnp.exp(cumulative)[..., None]
    decayed_keys = key_rows * jnp.exp(cumulative[..., -1:] - cumulative)[..., None]
    span_decay = jnp.exp(cumulative[..., -1])
    return (weights_w, updates_u, decayed_queries, decayed_keys, local_mix, span_decay)

def span_step(carried, pieces):
    weights_w, updates_u, decayed_queries, decayed_keys, local_mix, span_decay = pieces
    corrected = updates_u - jnp.einsum('bcd,bde->bce', weights_w, carried, precision=exact_mode)
    output = jnp.einsum('bcd,bde->bce', decayed_queries, carried, precision=exact_mode)
    output = output + jnp.einsum('bcj,bje->bce', local_mix, corrected, precision=exact_mode)
    carried = span_decay[:, None, None] * carried + jnp.einsum('bcd,bce->bde', decayed_keys, corrected, precision=exact_mode)
    return (carried, output)

def finish(outputs, norm_gain, live_rows):
    mean_square = lax.optimization_barrier(jnp.mean(outputs * outputs, axis=-1, keepdims=True))
    normed = outputs * lax.rsqrt(mean_square + norm_epsilon) * norm_gain.astype(jnp.float32)
    return jnp.where(live_rows[..., None], normed, 0.0).astype(jnp.bfloat16)

def restore(mixed_rows, expansions, key_heads):
    head_rows, length, value_dim = mixed_rows.shape
    return jnp.transpose(mixed_rows.reshape(expansions, key_heads, 2, length, value_dim), (0, 3, 1, 2, 4))

def reference(queries, keys, values, log_decay, write_rate, norm_gain, parent_cache, order, parent_owner, parent_slot, token_count):
    key_heads = queries.shape[2]
    parents = (parent_owner * PAR_DEV + parent_slot).astype(jnp.int32)

    def one_expansion(number):

        def pick_rows(tensor):
            return lax.dynamic_slice_in_dim(tensor, number, 1, 0)
        arranged = arrange(pick_rows(queries), pick_rows(keys), pick_rows(values), pick_rows(log_decay), pick_rows(write_rate), pick_rows(token_count), SPAN)
        query_rows, key_rows, value_rows, decay_rows, rate_rows, live_rows = arranged
        pieces = within_spans(query_rows, key_rows, value_rows, decay_rows, rate_rows)
        stacked = tuple((jnp.moveaxis(tensor, 1, 0) for tensor in pieces))
        initial = lax.dynamic_index_in_dim(parent_cache, parents[number], 0, keepdims=False)
        initial = initial.reshape(key_heads * 2, initial.shape[-2], initial.shape[-1])
        final_states, outputs = lax.scan(span_step, initial, stacked)
        outputs = jnp.moveaxis(outputs, 0, 1)
        outputs = outputs.reshape(key_heads * 2, -1, outputs.shape[-1])
        mixed_one = restore(finish(outputs, norm_gain, live_rows), 1, key_heads)
        return (mixed_one[0], final_states.reshape(key_heads, 2, final_states.shape[-2], final_states.shape[-1]))
    numbers = jnp.arange(queries.shape[0], dtype=jnp.int32)
    mixed_all, finals = lax.map(one_expansion, numbers)
    return (mixed_all, jnp.take(finals, order, axis=0))
```

```python
import functools

import jax
import jax.numpy as jnp
from jax import lax
from jax.experimental import pallas as pl
from jax.experimental.pallas import tpu as pltpu
from jax.sharding import PartitionSpec as P

norm_epsilon = 1e-06
BASE = 16
F32 = jnp.float32
BF16 = jnp.bfloat16
VMEM_BYTES = 56 * 1024 * 1024


def split(x):
    high = x.astype(BF16)
    low = (x - high.astype(F32)).astype(BF16)
    return high, low


def dot(a, b):
    return jnp.dot(a, b, preferred_element_type=F32)


def dot_nt(a, b):
    return lax.dot_general(a, b, (((1,), (1,)), ((), ())), preferred_element_type=F32)


def dot_tn(a, b):
    return lax.dot_general(a, b, (((0,), (0,)), ((), ())), preferred_element_type=F32)


def dot3(a, b):
    a_high, a_low = split(a)
    b_high, b_low = split(b)
    return dot3_split(a_high, a_low, b_high, b_low)


def dot3_split(a_high, a_low, b_high, b_low):
    return dot(a_high, b_high) + dot(a_low, b_high) + dot(a_high, b_low)


def prepare_kernel(count_ref, q_ref, k_ref, g_ref, b_ref, t_ref, m_ref, aux_ref,
                   q_rows, k_rows, a_rows):
    number = pl.program_id(0)
    live = count_ref[number]
    length, value_heads = g_ref.shape[1:]
    key_heads = value_heads // 2
    q_rows[...] = q_ref[0].astype(F32)
    k_rows[...] = k_ref[0].astype(F32)
    tokens = lax.broadcasted_iota(jnp.int32, (length, value_heads), 0)
    g = jnp.where(tokens < live, g_ref[0].astype(F32), 0.0)
    b = jnp.where(tokens < live, b_ref[0].astype(F32), 0.0)
    row = lax.broadcasted_iota(jnp.int32, (length, length), 0)
    col = lax.broadcasted_iota(jnp.int32, (length, length), 1)
    inclusive = row >= col
    strict = row > col
    diagonal = row == col
    ones_low = inclusive.astype(F32).astype(BF16)
    ones_up = (row <= col).astype(F32).astype(BF16)
    g_narrow = g.astype(BF16)
    g_col = dot(ones_low, g_narrow)
    g_row = dot_tn(g_narrow, ones_up)
    lane = lax.broadcasted_iota(jnp.int32, (BASE, length), 1)
    sub = lax.broadcasted_iota(jnp.int32, (BASE, length), 0)
    parts = length // BASE
    unit_cols = []
    compact = []
    for m in range(key_heads):
        q = q_rows[pl.ds(m, length, stride=key_heads), :].astype(BF16)
        k = k_rows[pl.ds(m, length, stride=key_heads), :].astype(BF16)
        both = dot_nt(jnp.concatenate([k, q], axis=0), k)
        kk = both[:length]
        qk = both[length:]
        squares = jnp.where(diagonal, kk, 0.0)
        n_row = lax.rsqrt(jnp.sum(squares, axis=0, keepdims=True) + norm_epsilon)
        n_col = lax.rsqrt(jnp.sum(squares, axis=1, keepdims=True) + norm_epsilon)
        unit_cols += [n_col, n_col]
        kk = kk * n_row * n_col
        qk = qk * n_row
        for r in range(2):
            h = 2 * m + r
            decay = jnp.exp(jnp.where(inclusive, g_col[:, h:h + 1] - g_row[h:h + 1, :], 0.0))
            m_ref[0, h] = jnp.where(inclusive, qk * decay, 0.0)
            a = jnp.where(strict, kk * decay * b[:, h:h + 1], 0.0)
            a_rows[h] = a
            piece = jnp.zeros((BASE, length), F32)
            for p in range(parts):
                piece = jnp.where(lane // BASE == p, a[p * BASE:(p + 1) * BASE], piece)
            compact.append(piece)
    inverses = [(lane % BASE == sub).astype(F32) for _ in range(value_heads)]
    for j in range(BASE - 1):
        index = (lane // BASE) * BASE + j
        for h in range(value_heads):
            factor = jnp.take_along_axis(compact[h], index, axis=1)
            inverses[h] = inverses[h] - factor * inverses[h][j:j + 1, :]
    for h in range(value_heads):
        a = a_rows[h]
        result = jnp.concatenate(
            [jnp.where(lane // BASE == p, inverses[h], 0.0) for p in range(parts)], axis=0
        )
        size = BASE
        while size < length:
            joined = (row // (2 * size) == col // (2 * size)) & (row // size != col // size)
            cross = jnp.where(joined, a, 0.0)
            result_high, result_low = split(result)
            cross_high, cross_low = split(cross)
            step = dot3_split(cross_high, cross_low, result_high, result_low)
            step_high, step_low = split(step)
            result = result - dot3_split(result_high, result_low, step_high, step_low)
            size *= 2
        t_ref[0, h] = result
    units = jnp.concatenate(unit_cols, axis=1)
    growth = jnp.exp(g_col)
    rest = jnp.exp(g_col[length - 1:length, :] - g_col) * units
    aux_ref[0] = jnp.concatenate([growth, b, b * growth * units, rest], axis=1)


def advance_kernel(ids_ref, parents_ref, count_ref, q_ref, k_ref, v_ref, t_ref, m_ref, aux_ref,
                   gain_ref, s_ref, old_ref, mixed_ref, state_ref,
                   q_rows, k_rows, v_rows, o_rows):
    del parents_ref, old_ref
    number = ids_ref[pl.program_id(0)]
    live = count_ref[number]
    value_heads, length = t_ref.shape[1:3]
    key_heads = value_heads // 2
    width = s_ref.shape[-1]
    q_rows[...] = q_ref[0].astype(F32)
    k_rows[...] = k_ref[0].astype(F32)
    v_rows[...] = v_ref[0].astype(F32)
    aux = aux_ref[0]
    gain = gain_ref[...].astype(F32)
    alive = lax.broadcasted_iota(jnp.int32, (length, width), 0) < live
    for m in range(key_heads):
        q = q_rows[pl.ds(m, length, stride=key_heads), :].astype(BF16)
        k = k_rows[pl.ds(m, length, stride=key_heads), :].astype(BF16)
        s = jnp.concatenate([s_ref[0, 2 * m], s_ref[0, 2 * m + 1]], axis=1)
        s_high, s_low = split(s)
        kq = jnp.concatenate([k, q], axis=0)
        applied = dot(jnp.concatenate([kq, kq], axis=1), jnp.concatenate([s_high, s_low], axis=0))
        updates = []
        for r in range(2):
            h = 2 * m + r
            growth = aux[:, h:h + 1]
            rate = aux[:, value_heads + h:value_heads + h + 1]
            scale = aux[:, 2 * value_heads + h:2 * value_heads + h + 1]
            rest = aux[:, 3 * value_heads + h:3 * value_heads + h + 1]
            v = v_rows[pl.ds(h, length, stride=value_heads), :]
            right = rate * v - scale * applied[:length, r * width:(r + 1) * width]
            fixed = dot3(t_ref[0, h], right)
            out = growth * applied[length:, r * width:(r + 1) * width] + dot3(m_ref[0, h], fixed)
            mean_square = jnp.mean(out * out, axis=1, keepdims=True)
            normed = out * lax.rsqrt(mean_square + norm_epsilon) * gain
            o_rows[pl.ds(h, length, stride=value_heads), :] = jnp.where(alive, normed, 0.0)
            updates.append(rest * fixed)
        update = jnp.concatenate(updates, axis=1)
        u_high, u_low = split(update)
        added = dot_tn(jnp.concatenate([k, k], axis=0), jnp.concatenate([u_high, u_low], axis=0))
        for r in range(2):
            h = 2 * m + r
            last = aux[length - 1:length, h:h + 1]
            state_ref[0, h] = last * s_ref[0, h] + added[:, r * width:(r + 1) * width]
    mixed_ref[0] = o_rows[...].astype(BF16)


def prepare(counts, queries, keys, decay, rate):
    expansions, length, value_heads = decay.shape
    rows, key_dim = queries.shape[1:]
    square = (expansions, value_heads, length, length)
    block = lambda shape: pl.BlockSpec((1,) + shape, lambda i, c: (i,) + (0,) * len(shape))
    work = expansions * value_heads
    return pl.pallas_call(
        prepare_kernel,
        out_shape=(
            jax.ShapeDtypeStruct(square, F32),
            jax.ShapeDtypeStruct(square, F32),
            jax.ShapeDtypeStruct((expansions, length, 4 * value_heads), F32),
        ),
        grid_spec=pltpu.PrefetchScalarGridSpec(
            num_scalar_prefetch=1,
            grid=(expansions,),
            in_specs=[
                block((rows, key_dim)),
                block((rows, key_dim)),
                block((length, value_heads)),
                block((length, value_heads)),
            ],
            out_specs=(
                block(square[1:]),
                block(square[1:]),
                block((length, 4 * value_heads)),
            ),
            scratch_shapes=[
                pltpu.VMEM((rows, key_dim), F32),
                pltpu.VMEM((rows, key_dim), F32),
                pltpu.VMEM((value_heads, length, length), F32),
            ],
        ),
        compiler_params=pltpu.CompilerParams(vmem_limit_bytes=VMEM_BYTES),
        cost_estimate=pl.CostEstimate(
            flops=work * 30 * 2 * length**3,
            bytes_accessed=work * 2 * 4 * length * length,
            transcendentals=work * length * length,
        ),
        name="prepare",
    )(counts, queries, keys, decay, rate)


def advance(ids, parents, counts, queries, keys, values, inverse, mixing, aux, gain, states, mixed):
    steps = ids.shape[0]
    value_heads, length = inverse.shape[1:3]
    rows, key_dim = queries.shape[1:]
    width = states.shape[-1]
    own = lambda shape: pl.BlockSpec(
        (1,) + shape, lambda i, ids, par, c: (ids[i],) + (0,) * len(shape)
    )
    state_block = (1, value_heads, key_dim, width)
    work = steps * value_heads
    return pl.pallas_call(
        advance_kernel,
        out_shape=(
            jax.ShapeDtypeStruct(mixed.shape, mixed.dtype),
            jax.ShapeDtypeStruct((steps,) + state_block[1:], F32),
        ),
        grid_spec=pltpu.PrefetchScalarGridSpec(
            num_scalar_prefetch=3,
            grid=(steps,),
            in_specs=[
                own((rows, key_dim)),
                own((rows, key_dim)),
                own((length * value_heads, width)),
                own((value_heads, length, length)),
                own((value_heads, length, length)),
                own((length, 4 * value_heads)),
                pl.BlockSpec((1, width), lambda i, ids, par, c: (0, 0)),
                pl.BlockSpec(state_block, lambda i, ids, par, c: (par[i], 0, 0, 0)),
                pl.BlockSpec(memory_space=pl.ANY),
            ],
            out_specs=(
                own((length * value_heads, width)),
                pl.BlockSpec(state_block, lambda i, ids, par, c: (i, 0, 0, 0)),
            ),
            scratch_shapes=[
                pltpu.VMEM((rows, key_dim), F32),
                pltpu.VMEM((rows, key_dim), F32),
                pltpu.VMEM((length * value_heads, width), F32),
                pltpu.VMEM((length * value_heads, width), F32),
            ],
        ),
        input_output_aliases={11: 0},
        compiler_params=pltpu.CompilerParams(vmem_limit_bytes=VMEM_BYTES),
        cost_estimate=pl.CostEstimate(
            flops=work * 12 * 2 * length**3,
            bytes_accessed=work * 5 * 4 * length * length,
            transcendentals=work * length,
        ),
        name="advance",
    )(ids, parents, counts, queries, keys, values, inverse, mixing, aux, gain, states, mixed)


def shards(queries, keys, values, log_decay, write_rate, norm_gain, parent_cache, order,
           parent_owner, parent_slot, token_count):
    seq_count = lax.axis_size("seq")
    me = lax.axis_index("seq")
    expansions, length, key_heads, key_dim = queries.shape
    value_heads = 2 * key_heads
    width = values.shape[-1]
    per_peer = expansions // seq_count
    cache_rows = parent_cache.shape[0]
    states = parent_cache.reshape(cache_rows, value_heads, key_dim, width)
    states = lax.all_gather(states, "seq", axis=0, tiled=True)
    start = me * expansions
    own = lambda table: lax.dynamic_slice_in_dim(table, start, expansions)
    counts = own(token_count)
    parents = own(parent_owner) * cache_rows + own(parent_slot)
    sends = lax.dynamic_slice_in_dim(
        order.reshape(seq_count, expansions), me * per_peer, per_peer, 1
    ) - start
    q = queries.reshape(expansions, length * key_heads, key_dim)
    k = keys.reshape(expansions, length * key_heads, key_dim)
    v = values.reshape(expansions, length * value_heads, width)
    decay = log_decay.reshape(expansions, length, value_heads)
    rate = write_rate.reshape(expansions, length, value_heads)
    inverse, mixing, aux = prepare(counts, q, k, decay, rate)
    mixed = jnp.zeros((expansions, length * value_heads, width), BF16)
    gain = norm_gain.reshape(1, width)
    final = jnp.zeros((expansions, value_heads, key_dim, width), F32)
    shifts = sorted(range(seq_count), key=lambda s: -min(s, seq_count - s))
    for shift in shifts:
        target = lax.rem(me + shift, seq_count)
        ids = lax.dynamic_index_in_dim(sends, target, 0, keepdims=False)
        mixed, chunk = advance(ids, jnp.take(parents, ids), counts, q, k, v, inverse, mixing, aux,
                               gain, states, mixed)
        if shift:
            chunk = lax.ppermute(
                chunk, "seq", [(d, (d + shift) % seq_count) for d in range(seq_count)]
            )
        source = lax.rem(me + seq_count - shift, seq_count)
        final = lax.dynamic_update_slice_in_dim(final, chunk, source * per_peer, 0)
    return (
        mixed.reshape(values.shape),
        final.reshape((expansions,) + parent_cache.shape[1:]),
    )


def solution(mesh):
    heads = ("head", "sub")
    rows = ("groups", "seq")
    placed = (
        P(rows, None, heads, None),
        P(rows, None, heads, None),
        P(rows, None, heads, None, None),
        P(rows, None, heads, None),
        P(rows, None, heads, None),
        P(),
        P(rows, heads, None, None, None),
        P("groups"),
        P("groups"),
        P("groups"),
        P("groups"),
    )
    return jax.shard_map(
        shards,
        mesh=mesh,
        in_specs=placed,
        out_specs=(P(rows, None, heads, None, None), P(rows, heads, None, None, None)),
        check_vma=False,
    )
```

```python
import functools

import jax
import jax.numpy as jnp
from jax import lax
from jax.experimental import pallas as pl
from jax.experimental.pallas import tpu as pltpu
from jax.sharding import PartitionSpec as P

norm_epsilon = 1e-06
BASE = 16
F32 = jnp.float32
BF16 = jnp.bfloat16
VMEM_BYTES = 56 * 1024 * 1024


def split(x):
    high = x.astype(BF16)
    low = (x - high.astype(F32)).astype(BF16)
    return high, low


def dot(a, b):
    return jnp.dot(a, b, preferred_element_type=F32)


def dot_nt(a, b):
    return lax.dot_general(a, b, (((1,), (1,)), ((), ())), preferred_element_type=F32)


def dot_tn(a, b):
    return lax.dot_general(a, b, (((0,), (0,)), ((), ())), preferred_element_type=F32)


def dot3(a, b):
    a_high, a_low = split(a)
    b_high, b_low = split(b)
    right = jnp.concatenate([b_high, b_low], axis=1)
    both = dot(jnp.concatenate([a_high, a_low], axis=1), jnp.concatenate([right, right], axis=0))
    width = b.shape[1]
    return both[:, :width] + both[:, width:]


CODE_BITS = 15
CODE_ROWS = 16


def store_codes(code_ref, number, state):
    rows = state.shape[0]
    largest = jnp.maximum(jnp.max(jnp.abs(state), axis=0, keepdims=True), 1e-30)
    power = jnp.ceil(jnp.log2(largest)) - CODE_BITS
    limit = float(2**CODE_BITS - 1)
    code = jnp.clip(jnp.round(state * jnp.exp2(-power)), -limit, limit)
    code_ref[0, number * rows:(number + 1) * rows, :] = code.astype(jnp.int32).astype(jnp.int16)
    return power


def store_powers(code_ref, powers):
    rows = code_ref.shape[1] - CODE_ROWS
    spare = jnp.zeros((CODE_ROWS - len(powers), code_ref.shape[2]), F32)
    table = jnp.concatenate(powers + [spare], axis=0)
    code_ref[0, rows:, :] = table.astype(jnp.int32).astype(jnp.int16)


def load_scales(code_ref):
    rows = code_ref.shape[1] - CODE_ROWS
    return jnp.exp2(code_ref[0, rows:, :].astype(jnp.int32).astype(F32))


def load_state(code_ref, scales, number, rows):
    code = code_ref[0, number * rows:(number + 1) * rows, :].astype(jnp.int32).astype(F32)
    return code * scales[number:number + 1, :]


def encode_kernel(state_ref, code_ref):
    heads = state_ref.shape[1]
    store_powers(code_ref, [store_codes(code_ref, h, state_ref[0, h]) for h in range(heads)])


def decode_kernel(place_ref, code_ref, *refs):
    del place_ref
    state_ref = refs[-1]
    heads, rows = state_ref.shape[1:3]
    scales = load_scales(code_ref)
    for h in range(heads):
        state_ref[0, h] = load_state(code_ref, scales, h, rows)


def prepare_kernel(ids_ref, count_ref, q_ref, k_ref, g_ref, b_ref, t_ref, m_ref, aux_ref,
                   q_rows, k_rows, a_rows):
    live = count_ref[ids_ref[pl.program_id(0)]]
    length, value_heads = g_ref.shape[1:]
    key_heads = value_heads // 2
    q_rows[...] = q_ref[0].astype(F32)
    k_rows[...] = k_ref[0].astype(F32)
    tokens = lax.broadcasted_iota(jnp.int32, (length, value_heads), 0)
    g = jnp.where(tokens < live, g_ref[0].astype(F32), 0.0)
    b = jnp.where(tokens < live, b_ref[0].astype(F32), 0.0)
    row = lax.broadcasted_iota(jnp.int32, (length, length), 0)
    col = lax.broadcasted_iota(jnp.int32, (length, length), 1)
    inclusive = row >= col
    strict = row > col
    diagonal = row == col
    ones_low = inclusive.astype(F32).astype(BF16)
    ones_up = (row <= col).astype(F32).astype(BF16)
    g_narrow = g.astype(BF16)
    g_col = dot(ones_low, g_narrow)
    g_row = dot_tn(g_narrow, ones_up)
    lane = lax.broadcasted_iota(jnp.int32, (BASE, length), 1)
    sub = lax.broadcasted_iota(jnp.int32, (BASE, length), 0)
    parts = length // BASE
    unit_cols = []
    compact = []
    for m in range(key_heads):
        q = q_rows[pl.ds(m, length, stride=key_heads), :].astype(BF16)
        k = k_rows[pl.ds(m, length, stride=key_heads), :].astype(BF16)
        both = dot_nt(jnp.concatenate([k, q], axis=0), k)
        kk = both[:length]
        qk = both[length:]
        squares = jnp.where(diagonal, kk, 0.0)
        n_row = lax.rsqrt(jnp.sum(squares, axis=0, keepdims=True) + norm_epsilon)
        n_col = lax.rsqrt(jnp.sum(squares, axis=1, keepdims=True) + norm_epsilon)
        unit_cols += [n_col, n_col]
        kk = kk * n_row * n_col
        qk = qk * n_row
        for r in range(2):
            h = 2 * m + r
            decay = jnp.exp(jnp.where(inclusive, g_col[:, h:h + 1] - g_row[h:h + 1, :], 0.0))
            m_ref[0, h] = jnp.where(inclusive, qk * decay, 0.0)
            a = jnp.where(strict, kk * decay * b[:, h:h + 1], 0.0)
            a_rows[h] = a
            piece = jnp.zeros((BASE, length), F32)
            for p in range(parts):
                piece = jnp.where(lane // BASE == p, a[p * BASE:(p + 1) * BASE], piece)
            compact.append(piece)
    inverses = [(lane % BASE == sub).astype(F32) for _ in range(value_heads)]
    for j in range(BASE - 1):
        index = (lane // BASE) * BASE + j
        for h in range(value_heads):
            factor = jnp.take_along_axis(compact[h], index, axis=1)
            inverses[h] = inverses[h] - factor * inverses[h][j:j + 1, :]
    block_masks = [lane // BASE == p for p in range(parts)]
    levels = []
    size = BASE
    while size < length:
        levels.append((size, range(size, length, 2 * size)))
        size *= 2
    for h in range(value_heads):
        blocks = [jnp.where(block_masks[p], inverses[h], 0.0) for p in range(parts)]
        result = jnp.concatenate(blocks, axis=0)
        for size, starts in levels:
            lower = [
                jnp.where(
                    lax.broadcasted_iota(jnp.int32, (size, length), 1) // size == start // size - 1,
                    a_rows[h, start:start + size, :],
                    0.0,
                )
                for start in starts
            ]
            step = dot3(jnp.concatenate(lower, axis=0), result)
            empty = jnp.zeros((size, length), F32)
            spread = []
            for n in range(len(starts)):
                spread += [empty, step[n * size:(n + 1) * size]]
            odd = jnp.concatenate([result[start:start + size] for start in starts], axis=0)
            odd = odd - dot3(odd, jnp.concatenate(spread, axis=0))
            joint = []
            for n, start in enumerate(starts):
                joint += [result[start - size:start], odd[n * size:(n + 1) * size]]
            result = jnp.concatenate(joint, axis=0)
        t_ref[0, h] = result
    units = jnp.concatenate(unit_cols, axis=1)
    growth = jnp.exp(g_col)
    rest = jnp.exp(g_col[length - 1:length, :] - g_col) * units
    aux_ref[0] = jnp.concatenate([growth, b, b * growth * units, rest], axis=1)


def advance_kernel(coded, ids_ref, parents_ref, count_ref, place_ref, q_ref, k_ref, v_ref, t_ref,
                   m_ref, aux_ref, gain_ref, s_ref, *refs):
    del parents_ref, place_ref
    mixed_ref, state_ref, q_rows, k_rows, v_rows, o_rows = refs[-6:]
    number = ids_ref[pl.program_id(0)]
    live = count_ref[number]
    value_heads, length = t_ref.shape[1:3]
    key_heads = value_heads // 2
    width = s_ref.shape[-1]
    key_dim = k_ref.shape[-1]
    scales = load_scales(s_ref)
    powers = []
    q_rows[...] = q_ref[0].astype(F32)
    k_rows[...] = k_ref[0].astype(F32)
    v_rows[...] = v_ref[0].astype(F32)
    aux = aux_ref[0]
    gain = gain_ref[...].astype(F32)
    alive = lax.broadcasted_iota(jnp.int32, (length, width), 0) < live
    for m in range(key_heads):
        q = q_rows[pl.ds(m, length, stride=key_heads), :].astype(BF16)
        k = k_rows[pl.ds(m, length, stride=key_heads), :].astype(BF16)
        states = [load_state(s_ref, scales, 2 * m + r, key_dim) for r in range(2)]
        s = jnp.concatenate(states, axis=1)
        s_high, s_low = split(s)
        kq = jnp.concatenate([k, q], axis=0)
        applied = dot(jnp.concatenate([kq, kq], axis=1), jnp.concatenate([s_high, s_low], axis=0))
        updates = []
        for r in range(2):
            h = 2 * m + r
            growth = aux[:, h:h + 1]
            rate = aux[:, value_heads + h:value_heads + h + 1]
            scale = aux[:, 2 * value_heads + h:2 * value_heads + h + 1]
            rest = aux[:, 3 * value_heads + h:3 * value_heads + h + 1]
            v = v_rows[pl.ds(h, length, stride=value_heads), :]
            right = rate * v - scale * applied[:length, r * width:(r + 1) * width]
            fixed = dot3(t_ref[0, h], right)
            out = growth * applied[length:, r * width:(r + 1) * width] + dot3(m_ref[0, h], fixed)
            mean_square = jnp.mean(out * out, axis=1, keepdims=True)
            normed = out * lax.rsqrt(mean_square + norm_epsilon) * gain
            o_rows[pl.ds(h, length, stride=value_heads), :] = jnp.where(alive, normed, 0.0)
            updates.append(rest * fixed)
        update = jnp.concatenate(updates, axis=1)
        u_high, u_low = split(update)
        added = dot_tn(jnp.concatenate([k, k], axis=0), jnp.concatenate([u_high, u_low], axis=0))
        for r in range(2):
            h = 2 * m + r
            last = aux[length - 1:length, h:h + 1]
            state = last * states[r] + added[:, r * width:(r + 1) * width]
            if coded:
                powers.append(store_codes(state_ref, h, state))
            else:
                state_ref[0, h] = state
    if coded:
        store_powers(state_ref, powers)
    mixed_ref[0] = o_rows[...].astype(BF16)


def prepare(ids, counts, queries, keys, decay, rate):
    expansions = ids.shape[0]
    length, value_heads = decay.shape[1:]
    rows, key_dim = queries.shape[1:]
    square = (expansions, value_heads, length, length)
    own = lambda shape: pl.BlockSpec((1,) + shape, lambda i, ids, c: (ids[i],) + (0,) * len(shape))
    block = lambda shape: pl.BlockSpec((1,) + shape, lambda i, ids, c: (i,) + (0,) * len(shape))
    work = expansions * value_heads
    return pl.pallas_call(
        prepare_kernel,
        out_shape=(
            jax.ShapeDtypeStruct(square, F32),
            jax.ShapeDtypeStruct(square, F32),
            jax.ShapeDtypeStruct((expansions, length, 4 * value_heads), F32),
        ),
        grid_spec=pltpu.PrefetchScalarGridSpec(
            num_scalar_prefetch=2,
            grid=(expansions,),
            in_specs=[
                own((rows, key_dim)),
                own((rows, key_dim)),
                own((length, value_heads)),
                own((length, value_heads)),
            ],
            out_specs=(
                block(square[1:]),
                block(square[1:]),
                block((length, 4 * value_heads)),
            ),
            scratch_shapes=[
                pltpu.VMEM((rows, key_dim), F32),
                pltpu.VMEM((rows, key_dim), F32),
                pltpu.VMEM((value_heads, length, length), F32),
            ],
        ),
        compiler_params=pltpu.CompilerParams(vmem_limit_bytes=VMEM_BYTES),
        cost_estimate=pl.CostEstimate(
            flops=work * 30 * 2 * length**3,
            bytes_accessed=work * 2 * 4 * length * length,
            transcendentals=work * length * length,
        ),
        name="prepare",
    )(ids, counts, queries, keys, decay, rate)


def encode(states):
    count, heads, key_dim, width = states.shape
    rows = heads * key_dim + CODE_ROWS
    return pl.pallas_call(
        encode_kernel,
        out_shape=jax.ShapeDtypeStruct((count, rows, width), jnp.int16),
        grid=(count,),
        in_specs=[pl.BlockSpec((1, heads, key_dim, width), lambda i: (i, 0, 0, 0))],
        out_specs=pl.BlockSpec((1, rows, width), lambda i: (i, 0, 0)),
        compiler_params=pltpu.CompilerParams(vmem_limit_bytes=VMEM_BYTES),
        name="encode",
    )(states)


def decode(place, codes, final):
    count, rows, width = codes.shape
    heads, key_dim = final.shape[1:3]
    return pl.pallas_call(
        decode_kernel,
        out_shape=jax.ShapeDtypeStruct(final.shape, final.dtype),
        grid_spec=pltpu.PrefetchScalarGridSpec(
            num_scalar_prefetch=1,
            grid=(count,),
            in_specs=[
                pl.BlockSpec((1, rows, width), lambda i, place: (i, 0, 0)),
                pl.BlockSpec(memory_space=pl.ANY),
            ],
            out_specs=pl.BlockSpec(
                (1, heads, key_dim, width), lambda i, place: (place[0] + i, 0, 0, 0)
            ),
        ),
        input_output_aliases={2: 0},
        compiler_params=pltpu.CompilerParams(vmem_limit_bytes=VMEM_BYTES),
        name="decode",
    )(place, codes, final)


def advance(ids, parents, counts, place, first, queries, keys, values, inverse, mixing, aux, gain,
            states, mixed, coded):
    steps = ids.shape[0]
    expansions = queries.shape[0]
    value_heads, length = inverse.shape[1:3]
    rows, key_dim = queries.shape[1:]
    width = values.shape[-1]
    state_rows = states.shape[1]
    own = lambda shape: pl.BlockSpec(
        (1,) + shape, lambda i, ids, par, c, p: (ids[i],) + (0,) * len(shape)
    )
    step = lambda shape: pl.BlockSpec(
        (1,) + shape, lambda i, ids, par, c, p: (first + i,) + (0,) * len(shape)
    )
    if coded:
        state_shape = jax.ShapeDtypeStruct((steps, state_rows, width), jnp.int16)
        state_spec = pl.BlockSpec((1, state_rows, width), lambda i, ids, par, c, p: (i, 0, 0))
    else:
        state_shape = jax.ShapeDtypeStruct((expansions, value_heads, key_dim, width), F32)
        state_spec = pl.BlockSpec(
            (1, value_heads, key_dim, width), lambda i, ids, par, c, p: (p[0] + i, 0, 0, 0)
        )
    in_specs = [
        own((rows, key_dim)),
        own((rows, key_dim)),
        own((length * value_heads, width)),
        step((value_heads, length, length)),
        step((value_heads, length, length)),
        step((length, 4 * value_heads)),
        pl.BlockSpec((1, width), lambda i, ids, par, c, p: (0, 0)),
        pl.BlockSpec((1, state_rows, width), lambda i, ids, par, c, p: (par[i], 0, 0)),
    ]
    operands = [ids, parents, counts, place, queries, keys, values, inverse, mixing, aux, gain, states]
    aliases = {}
    if mixed is not None:
        aliases = {len(operands): 0}
        operands.append(mixed)
        in_specs.append(pl.BlockSpec(memory_space=pl.ANY))
    work = steps * value_heads
    return pl.pallas_call(
        functools.partial(advance_kernel, coded),
        out_shape=(jax.ShapeDtypeStruct(values.shape, BF16), state_shape),
        grid_spec=pltpu.PrefetchScalarGridSpec(
            num_scalar_prefetch=4,
            grid=(steps,),
            in_specs=in_specs,
            out_specs=(own((length * value_heads, width)), state_spec),
            scratch_shapes=[
                pltpu.VMEM((rows, key_dim), F32),
                pltpu.VMEM((rows, key_dim), F32),
                pltpu.VMEM((length * value_heads, width), F32),
                pltpu.VMEM((length * value_heads, width), F32),
            ],
        ),
        input_output_aliases=aliases,
        compiler_params=pltpu.CompilerParams(vmem_limit_bytes=VMEM_BYTES),
        cost_estimate=pl.CostEstimate(
            flops=work * 12 * 2 * length**3,
            bytes_accessed=work * 5 * 4 * length * length,
            transcendentals=work * length,
        ),
        name="advance",
    )(*operands)


def shards(queries, keys, values, log_decay, write_rate, norm_gain, parent_cache, order,
           parent_owner, parent_slot, token_count):
    seq_count = lax.axis_size("seq")
    me = lax.axis_index("seq")
    expansions, length, key_heads, key_dim = queries.shape
    value_heads = 2 * key_heads
    width = values.shape[-1]
    per_peer = expansions // seq_count
    cache_rows = parent_cache.shape[0]
    codes = encode(parent_cache.reshape(cache_rows, value_heads, key_dim, width))
    states = lax.all_gather(codes, "seq", axis=0, tiled=True)
    start = me * expansions
    own = lambda table: lax.dynamic_slice_in_dim(table, start, expansions)
    counts = own(token_count)
    parents = own(parent_owner) * cache_rows + own(parent_slot)
    sends = lax.dynamic_slice_in_dim(
        order.reshape(seq_count, expansions), me * per_peer, per_peer, 1
    ) - start
    shifts = sorted(range(seq_count), key=lambda s: -min(s, seq_count - s))
    targets = lax.rem(me + jnp.array(shifts, jnp.int32), seq_count)
    ids = jnp.take(sends, targets, axis=0).reshape(-1)
    parents = jnp.take(parents, ids)
    remote = expansions - per_peer
    q = queries.reshape(expansions, length * key_heads, key_dim)
    k = keys.reshape(expansions, length * key_heads, key_dim)
    v = values.reshape(expansions, length * value_heads, width)
    decay = log_decay.reshape(expansions, length, value_heads)
    rate = write_rate.reshape(expansions, length, value_heads)
    gain = norm_gain.reshape(1, width)
    pieces = prepare(ids[:remote], counts, q, k, decay, rate)
    mixed = None
    arriving = []
    for at, shift in enumerate(shifts):
        first = at * per_peer
        if not shift:
            late, _ = lax.optimization_barrier((ids[remote:], codes))
            pieces = prepare(late, counts, q, k, decay, rate)
            first = 0
        here = slice(at * per_peer, (at + 1) * per_peer)
        place = (lax.rem(me + seq_count - shift, seq_count) * per_peer).reshape(1)
        mixed, codes = advance(ids[here], parents[here], counts, place, first, q, k, v, *pieces,
                               gain, states, mixed, bool(shift))
        if shift:
            pairs = [(d, (d + shift) % seq_count) for d in range(seq_count)]
            arriving.append((place, lax.ppermute(codes, "seq", pairs)))
    final = codes
    for place, codes in arriving:
        final = decode(place, codes, final)
    return (
        mixed.reshape(values.shape),
        final.reshape((expansions,) + parent_cache.shape[1:]),
    )


def solution(mesh):
    heads = ("head", "sub")
    rows = ("groups", "seq")
    placed = (
        P(rows, None, heads, None),
        P(rows, None, heads, None),
        P(rows, None, heads, None, None),
        P(rows, None, heads, None),
        P(rows, None, heads, None),
        P(),
        P(rows, heads, None, None, None),
        P("groups"),
        P("groups"),
        P("groups"),
        P("groups"),
    )
    return jax.shard_map(
        shards,
        mesh=mesh,
        in_specs=placed,
        out_specs=(P(rows, None, heads, None, None), P(rows, heads, None, None, None)),
        check_vma=False,
    )
```

```python
import functools

import jax
import jax.numpy as jnp
from jax import lax
from jax.experimental import pallas as pl
from jax.experimental.pallas import tpu as pltpu
from jax.sharding import PartitionSpec as P

norm_epsilon = 1e-06
BASE = 16
F32 = jnp.float32
BF16 = jnp.bfloat16
VMEM_BYTES = 56 * 1024 * 1024


def split(x):
    high = x.astype(BF16)
    low = (x - high.astype(F32)).astype(BF16)
    return high, low


def dot(a, b):
    return jnp.dot(a, b, preferred_element_type=F32)


def dot_nt(a, b):
    return lax.dot_general(a, b, (((1,), (1,)), ((), ())), preferred_element_type=F32)


def dot_tn(a, b):
    return lax.dot_general(a, b, (((0,), (0,)), ((), ())), preferred_element_type=F32)


def dot3(a, b):
    a_high, a_low = split(a)
    b_high, b_low = split(b)
    right = jnp.concatenate([b_high, b_low], axis=1)
    both = dot(jnp.concatenate([a_high, a_low], axis=1), jnp.concatenate([right, right], axis=0))
    width = b.shape[1]
    return both[:, :width] + both[:, width:]


CODE_BITS = 15
CODE_ROWS = 8


def code_state(state):
    largest = jnp.maximum(jnp.max(jnp.abs(state), axis=0, keepdims=True), 1e-30)
    power = jnp.ceil(jnp.log2(largest)) - CODE_BITS
    limit = float(2**CODE_BITS - 1)
    code = jnp.clip(jnp.round(state * jnp.exp2(-power)), -limit, limit)
    return code.astype(jnp.int32), power.astype(jnp.int32)


def store_pair(code_ref, pair, states):
    (low, low_power), (high, high_power) = [code_state(state) for state in states]
    rows = low.shape[0]
    code_ref[0, pair * rows:(pair + 1) * rows, :] = (high << 16) | (low & 0xFFFF)
    return [low_power, high_power]


def store_powers(code_ref, powers):
    rows = code_ref.shape[1] - CODE_ROWS
    spare = [jnp.zeros_like(powers[0])] * (CODE_ROWS - len(powers))
    code_ref[0, rows:, :] = jnp.concatenate(powers + spare, axis=0)


def load_scales(code_ref):
    rows = code_ref.shape[1] - CODE_ROWS
    return jnp.exp2(code_ref[0, rows:, :].astype(F32))


def load_pair(code_ref, scales, pair, rows):
    word = code_ref[0, pair * rows:(pair + 1) * rows, :]
    codes = [(word << 16) >> 16, word >> 16]
    return [c.astype(F32) * scales[2 * pair + r:2 * pair + r + 1, :] for r, c in enumerate(codes)]


def encode_kernel(state_ref, code_ref):
    powers = []
    for m in range(state_ref.shape[1] // 2):
        powers += store_pair(code_ref, m, [state_ref[0, 2 * m], state_ref[0, 2 * m + 1]])
    store_powers(code_ref, powers)


def decode_kernel(place_ref, code_ref, *refs):
    del place_ref
    state_ref = refs[-1]
    heads, rows = state_ref.shape[1:3]
    scales = load_scales(code_ref)
    for m in range(heads // 2):
        state_ref[0, 2 * m], state_ref[0, 2 * m + 1] = load_pair(code_ref, scales, m, rows)


def prepare_kernel(ids_ref, count_ref, q_ref, k_ref, g_ref, b_ref, t_ref, m_ref, aux_ref,
                   q_rows, k_rows, a_rows):
    live = count_ref[ids_ref[pl.program_id(0)]]
    length, value_heads = g_ref.shape[1:]
    key_heads = value_heads // 2
    q_rows[...] = q_ref[0].astype(F32)
    k_rows[...] = k_ref[0].astype(F32)
    tokens = lax.broadcasted_iota(jnp.int32, (length, value_heads), 0)
    g = jnp.where(tokens < live, g_ref[0].astype(F32), 0.0)
    b = jnp.where(tokens < live, b_ref[0].astype(F32), 0.0)
    row = lax.broadcasted_iota(jnp.int32, (length, length), 0)
    col = lax.broadcasted_iota(jnp.int32, (length, length), 1)
    inclusive = row >= col
    strict = row > col
    diagonal = row == col
    ones_low = inclusive.astype(F32).astype(BF16)
    ones_up = (row <= col).astype(F32).astype(BF16)
    g_narrow = g.astype(BF16)
    g_col = dot(ones_low, g_narrow)
    g_row = dot_tn(g_narrow, ones_up)
    lane = lax.broadcasted_iota(jnp.int32, (BASE, length), 1)
    sub = lax.broadcasted_iota(jnp.int32, (BASE, length), 0)
    parts = length // BASE
    unit_cols = []
    compact = []
    for m in range(key_heads):
        q = q_rows[pl.ds(m, length, stride=key_heads), :].astype(BF16)
        k = k_rows[pl.ds(m, length, stride=key_heads), :].astype(BF16)
        both = dot_nt(jnp.concatenate([k, q], axis=0), k)
        kk = both[:length]
        qk = both[length:]
        squares = jnp.where(diagonal, kk, 0.0)
        n_row = lax.rsqrt(jnp.sum(squares, axis=0, keepdims=True) + norm_epsilon)
        n_col = lax.rsqrt(jnp.sum(squares, axis=1, keepdims=True) + norm_epsilon)
        unit_cols += [n_col, n_col]
        kk = kk * n_row * n_col
        qk = qk * n_row
        for r in range(2):
            h = 2 * m + r
            decay = jnp.exp(jnp.where(inclusive, g_col[:, h:h + 1] - g_row[h:h + 1, :], 0.0))
            m_ref[0, h] = jnp.where(inclusive, qk * decay, 0.0)
            a = jnp.where(strict, kk * decay * b[:, h:h + 1], 0.0)
            a_rows[h] = a
            piece = jnp.zeros((BASE, length), F32)
            for p in range(parts):
                piece = jnp.where(lane // BASE == p, a[p * BASE:(p + 1) * BASE], piece)
            compact.append(piece)
    inverses = [(lane % BASE == sub).astype(F32) for _ in range(value_heads)]
    for j in range(BASE - 1):
        index = (lane // BASE) * BASE + j
        for h in range(value_heads):
            factor = jnp.take_along_axis(compact[h], index, axis=1)
            inverses[h] = inverses[h] - factor * inverses[h][j:j + 1, :]
    block_masks = [lane // BASE == p for p in range(parts)]
    levels = []
    size = BASE
    while size < length:
        levels.append((size, range(size, length, 2 * size)))
        size *= 2
    for h in range(value_heads):
        blocks = [jnp.where(block_masks[p], inverses[h], 0.0) for p in range(parts)]
        result = jnp.concatenate(blocks, axis=0)
        for size, starts in levels:
            lower = [
                jnp.where(
                    lax.broadcasted_iota(jnp.int32, (size, length), 1) // size == start // size - 1,
                    a_rows[h, start:start + size, :],
                    0.0,
                )
                for start in starts
            ]
            step = dot3(jnp.concatenate(lower, axis=0), result)
            empty = jnp.zeros((size, length), F32)
            spread = []
            for n in range(len(starts)):
                spread += [empty, step[n * size:(n + 1) * size]]
            odd = jnp.concatenate([result[start:start + size] for start in starts], axis=0)
            odd = odd - dot3(odd, jnp.concatenate(spread, axis=0))
            joint = []
            for n, start in enumerate(starts):
                joint += [result[start - size:start], odd[n * size:(n + 1) * size]]
            result = jnp.concatenate(joint, axis=0)
        t_ref[0, h] = result
    units = jnp.concatenate(unit_cols, axis=1)
    growth = jnp.exp(g_col)
    rest = jnp.exp(g_col[length - 1:length, :] - g_col) * units
    aux_ref[0] = jnp.concatenate([growth, b, b * growth * units, rest], axis=1)


def advance_kernel(coded, ids_ref, parents_ref, count_ref, place_ref, q_ref, k_ref, v_ref, t_ref,
                   m_ref, aux_ref, gain_ref, s_ref, *refs):
    del parents_ref, place_ref
    mixed_ref, state_ref, q_rows, k_rows, v_rows, o_rows = refs[-6:]
    number = ids_ref[pl.program_id(0)]
    live = count_ref[number]
    value_heads, length = t_ref.shape[1:3]
    key_heads = value_heads // 2
    width = s_ref.shape[-1]
    key_dim = k_ref.shape[-1]
    scales = load_scales(s_ref)
    powers = []
    q_rows[...] = q_ref[0].astype(F32)
    k_rows[...] = k_ref[0].astype(F32)
    v_rows[...] = v_ref[0].astype(F32)
    aux = aux_ref[0]
    gain = gain_ref[...].astype(F32)
    alive = lax.broadcasted_iota(jnp.int32, (length, width), 0) < live
    for m in range(key_heads):
        q = q_rows[pl.ds(m, length, stride=key_heads), :].astype(BF16)
        k = k_rows[pl.ds(m, length, stride=key_heads), :].astype(BF16)
        states = load_pair(s_ref, scales, m, key_dim)
        s = jnp.concatenate(states, axis=1)
        s_high, s_low = split(s)
        kq = jnp.concatenate([k, q], axis=0)
        applied = dot(jnp.concatenate([kq, kq], axis=1), jnp.concatenate([s_high, s_low], axis=0))
        updates = []
        for r in range(2):
            h = 2 * m + r
            growth = aux[:, h:h + 1]
            rate = aux[:, value_heads + h:value_heads + h + 1]
            scale = aux[:, 2 * value_heads + h:2 * value_heads + h + 1]
            rest = aux[:, 3 * value_heads + h:3 * value_heads + h + 1]
            v = v_rows[pl.ds(h, length, stride=value_heads), :]
            right = rate * v - scale * applied[:length, r * width:(r + 1) * width]
            fixed = dot3(t_ref[0, h], right)
            out = growth * applied[length:, r * width:(r + 1) * width] + dot3(m_ref[0, h], fixed)
            mean_square = jnp.mean(out * out, axis=1, keepdims=True)
            normed = out * lax.rsqrt(mean_square + norm_epsilon) * gain
            o_rows[pl.ds(h, length, stride=value_heads), :] = jnp.where(alive, normed, 0.0)
            updates.append(rest * fixed)
        update = jnp.concatenate(updates, axis=1)
        u_high, u_low = split(update)
        added = dot_tn(jnp.concatenate([k, k], axis=0), jnp.concatenate([u_high, u_low], axis=0))
        later = []
        for r in range(2):
            h = 2 * m + r
            last = aux[length - 1:length, h:h + 1]
            later.append(last * states[r] + added[:, r * width:(r + 1) * width])
        if coded:
            powers += store_pair(state_ref, m, later)
        else:
            state_ref[0, 2 * m], state_ref[0, 2 * m + 1] = later
    if coded:
        store_powers(state_ref, powers)
    mixed_ref[0] = o_rows[...].astype(BF16)


def prepare(ids, counts, queries, keys, decay, rate):
    expansions = ids.shape[0]
    length, value_heads = decay.shape[1:]
    rows, key_dim = queries.shape[1:]
    square = (expansions, value_heads, length, length)
    own = lambda shape: pl.BlockSpec((1,) + shape, lambda i, ids, c: (ids[i],) + (0,) * len(shape))
    block = lambda shape: pl.BlockSpec((1,) + shape, lambda i, ids, c: (i,) + (0,) * len(shape))
    work = expansions * value_heads
    return pl.pallas_call(
        prepare_kernel,
        out_shape=(
            jax.ShapeDtypeStruct(square, F32),
            jax.ShapeDtypeStruct(square, F32),
            jax.ShapeDtypeStruct((expansions, length, 4 * value_heads), F32),
        ),
        grid_spec=pltpu.PrefetchScalarGridSpec(
            num_scalar_prefetch=2,
            grid=(expansions,),
            in_specs=[
                own((rows, key_dim)),
                own((rows, key_dim)),
                own((length, value_heads)),
                own((length, value_heads)),
            ],
            out_specs=(
                block(square[1:]),
                block(square[1:]),
                block((length, 4 * value_heads)),
            ),
            scratch_shapes=[
                pltpu.VMEM((rows, key_dim), F32),
                pltpu.VMEM((rows, key_dim), F32),
                pltpu.VMEM((value_heads, length, length), F32),
            ],
        ),
        compiler_params=pltpu.CompilerParams(vmem_limit_bytes=VMEM_BYTES),
        cost_estimate=pl.CostEstimate(
            flops=work * 30 * 2 * length**3,
            bytes_accessed=work * 2 * 4 * length * length,
            transcendentals=work * length * length,
        ),
        name="prepare",
    )(ids, counts, queries, keys, decay, rate)


def encode(states):
    count, heads, key_dim, width = states.shape
    rows = heads // 2 * key_dim + CODE_ROWS
    return pl.pallas_call(
        encode_kernel,
        out_shape=jax.ShapeDtypeStruct((count, rows, width), jnp.int32),
        grid=(count,),
        in_specs=[pl.BlockSpec((1, heads, key_dim, width), lambda i: (i, 0, 0, 0))],
        out_specs=pl.BlockSpec((1, rows, width), lambda i: (i, 0, 0)),
        compiler_params=pltpu.CompilerParams(vmem_limit_bytes=VMEM_BYTES),
        name="encode",
    )(states)


def decode(place, codes, final):
    count, rows, width = codes.shape
    heads, key_dim = final.shape[1:3]
    return pl.pallas_call(
        decode_kernel,
        out_shape=jax.ShapeDtypeStruct(final.shape, final.dtype),
        grid_spec=pltpu.PrefetchScalarGridSpec(
            num_scalar_prefetch=1,
            grid=(count,),
            in_specs=[
                pl.BlockSpec((1, rows, width), lambda i, place: (i, 0, 0)),
                pl.BlockSpec(memory_space=pl.ANY),
            ],
            out_specs=pl.BlockSpec(
                (1, heads, key_dim, width), lambda i, place: (place[0] + i, 0, 0, 0)
            ),
        ),
        input_output_aliases={2: 0},
        compiler_params=pltpu.CompilerParams(vmem_limit_bytes=VMEM_BYTES),
        name="decode",
    )(place, codes, final)


def advance(ids, parents, counts, place, first, queries, keys, values, inverse, mixing, aux, gain,
            states, mixed, coded):
    steps = ids.shape[0]
    expansions = queries.shape[0]
    value_heads, length = inverse.shape[1:3]
    rows, key_dim = queries.shape[1:]
    width = values.shape[-1]
    state_rows = states.shape[1]
    own = lambda shape: pl.BlockSpec(
        (1,) + shape, lambda i, ids, par, c, p: (ids[i],) + (0,) * len(shape)
    )
    step = lambda shape: pl.BlockSpec(
        (1,) + shape, lambda i, ids, par, c, p: (first + i,) + (0,) * len(shape)
    )
    if coded:
        state_shape = jax.ShapeDtypeStruct((steps, state_rows, width), jnp.int32)
        state_spec = pl.BlockSpec((1, state_rows, width), lambda i, ids, par, c, p: (i, 0, 0))
    else:
        state_shape = jax.ShapeDtypeStruct((expansions, value_heads, key_dim, width), F32)
        state_spec = pl.BlockSpec(
            (1, value_heads, key_dim, width), lambda i, ids, par, c, p: (p[0] + i, 0, 0, 0)
        )
    in_specs = [
        own((rows, key_dim)),
        own((rows, key_dim)),
        own((length * value_heads, width)),
        step((value_heads, length, length)),
        step((value_heads, length, length)),
        step((length, 4 * value_heads)),
        pl.BlockSpec((1, width), lambda i, ids, par, c, p: (0, 0)),
        pl.BlockSpec((1, state_rows, width), lambda i, ids, par, c, p: (par[i], 0, 0)),
    ]
    operands = [ids, parents, counts, place, queries, keys, values, inverse, mixing, aux, gain, states]
    aliases = {}
    if mixed is not None:
        aliases = {len(operands): 0}
        operands.append(mixed)
        in_specs.append(pl.BlockSpec(memory_space=pl.ANY))
    work = steps * value_heads
    return pl.pallas_call(
        functools.partial(advance_kernel, coded),
        out_shape=(jax.ShapeDtypeStruct(values.shape, BF16), state_shape),
        grid_spec=pltpu.PrefetchScalarGridSpec(
            num_scalar_prefetch=4,
            grid=(steps,),
            in_specs=in_specs,
            out_specs=(own((length * value_heads, width)), state_spec),
            scratch_shapes=[
                pltpu.VMEM((rows, key_dim), F32),
                pltpu.VMEM((rows, key_dim), F32),
                pltpu.VMEM((length * value_heads, width), F32),
                pltpu.VMEM((length * value_heads, width), F32),
            ],
        ),
        input_output_aliases=aliases,
        compiler_params=pltpu.CompilerParams(vmem_limit_bytes=VMEM_BYTES),
        cost_estimate=pl.CostEstimate(
            flops=work * 12 * 2 * length**3,
            bytes_accessed=work * 5 * 4 * length * length,
            transcendentals=work * length,
        ),
        name="advance",
    )(*operands)


def shards(queries, keys, values, log_decay, write_rate, norm_gain, parent_cache, order,
           parent_owner, parent_slot, token_count):
    seq_count = lax.axis_size("seq")
    me = lax.axis_index("seq")
    expansions, length, key_heads, key_dim = queries.shape
    value_heads = 2 * key_heads
    width = values.shape[-1]
    per_peer = expansions // seq_count
    cache_rows = parent_cache.shape[0]
    codes = encode(parent_cache.reshape(cache_rows, value_heads, key_dim, width))
    states = lax.all_gather(codes, "seq", axis=0, tiled=True)
    start = me * expansions
    own = lambda table: lax.dynamic_slice_in_dim(table, start, expansions)
    counts = own(token_count)
    parents = own(parent_owner) * cache_rows + own(parent_slot)
    sends = lax.dynamic_slice_in_dim(
        order.reshape(seq_count, expansions), me * per_peer, per_peer, 1
    ) - start
    shifts = sorted(range(seq_count), key=lambda s: -min(s, seq_count - s))
    targets = lax.rem(me + jnp.array(shifts, jnp.int32), seq_count)
    ids = jnp.take(sends, targets, axis=0).reshape(-1)
    parents = jnp.take(parents, ids)
    remote = expansions - per_peer
    q = queries.reshape(expansions, length * key_heads, key_dim)
    k = keys.reshape(expansions, length * key_heads, key_dim)
    v = values.reshape(expansions, length * value_heads, width)
    decay = log_decay.reshape(expansions, length, value_heads)
    rate = write_rate.reshape(expansions, length, value_heads)
    gain = norm_gain.reshape(1, width)
    pieces = prepare(ids[:remote], counts, q, k, decay, rate)
    mixed = None
    arriving = []
    for at, shift in enumerate(shifts):
        first = at * per_peer
        if not shift:
            late, _ = lax.optimization_barrier((ids[remote:], codes))
            pieces = prepare(late, counts, q, k, decay, rate)
            first = 0
        here = slice(at * per_peer, (at + 1) * per_peer)
        place = (lax.rem(me + seq_count - shift, seq_count) * per_peer).reshape(1)
        mixed, codes = advance(ids[here], parents[here], counts, place, first, q, k, v, *pieces,
                               gain, states, mixed, bool(shift))
        if shift:
            pairs = [(d, (d + shift) % seq_count) for d in range(seq_count)]
            arriving.append((place, lax.ppermute(codes, "seq", pairs)))
    final = codes
    for place, codes in arriving:
        final = decode(place, codes, final)
    return (
        mixed.reshape(values.shape),
        final.reshape((expansions,) + parent_cache.shape[1:]),
    )


def solution(mesh):
    heads = ("head", "sub")
    rows = ("groups", "seq")
    placed = (
        P(rows, None, heads, None),
        P(rows, None, heads, None),
        P(rows, None, heads, None, None),
        P(rows, None, heads, None),
        P(rows, None, heads, None),
        P(),
        P(rows, heads, None, None, None),
        P("groups"),
        P("groups"),
        P("groups"),
        P("groups"),
    )
    return jax.shard_map(
        shards,
        mesh=mesh,
        in_specs=placed,
        out_specs=(P(rows, None, heads, None, None), P(rows, heads, None, None, None)),
        check_vma=False,
    )
```

```python
import functools

import jax
import jax.numpy as jnp
from jax import lax
from jax.experimental import pallas as pl
from jax.experimental.pallas import tpu as pltpu
from jax.sharding import PartitionSpec as P

norm_epsilon = 1e-06
BASE = 16
F32 = jnp.float32
BF16 = jnp.bfloat16
VMEM_BYTES = 56 * 1024 * 1024


def split(x):
    high = x.astype(BF16)
    low = (x - high.astype(F32)).astype(BF16)
    return high, low


def dot(a, b):
    return jnp.dot(a, b, preferred_element_type=F32)


def dot_nt(a, b):
    return lax.dot_general(a, b, (((1,), (1,)), ((), ())), preferred_element_type=F32)


def dot_tn(a, b):
    return lax.dot_general(a, b, (((0,), (0,)), ((), ())), preferred_element_type=F32)


def dot3(a, b):
    a_high, a_low = split(a)
    b_high, b_low = split(b)
    right = jnp.concatenate([b_high, b_low], axis=1)
    both = dot(jnp.concatenate([a_high, a_low], axis=1), jnp.concatenate([right, right], axis=0))
    width = b.shape[1]
    return both[:, :width] + both[:, width:]


CODE_BITS = 15
CODE_ROWS = 8


def code_state(state):
    largest = jnp.maximum(jnp.max(jnp.abs(state), axis=0, keepdims=True), 1e-30)
    power = jnp.ceil(jnp.log2(largest)) - CODE_BITS
    limit = float(2**CODE_BITS - 1)
    code = jnp.clip(jnp.round(state * jnp.exp2(-power)), -limit, limit)
    return code.astype(jnp.int32), power.astype(jnp.int32)


def store_pair(code_ref, pair, states):
    (low, low_power), (high, high_power) = [code_state(state) for state in states]
    rows = low.shape[0]
    code_ref[0, pair * rows:(pair + 1) * rows, :] = (high << 16) | (low & 0xFFFF)
    return [low_power, high_power]


def store_powers(code_ref, powers):
    rows = code_ref.shape[1] - CODE_ROWS
    spare = [jnp.zeros_like(powers[0])] * (CODE_ROWS - len(powers))
    code_ref[0, rows:, :] = jnp.concatenate(powers + spare, axis=0)


def load_scales(code_ref):
    rows = code_ref.shape[1] - CODE_ROWS
    return jnp.exp2(code_ref[0, rows:, :].astype(F32))


def load_pair(code_ref, scales, pair, rows):
    word = code_ref[0, pair * rows:(pair + 1) * rows, :]
    codes = [(word << 16) >> 16, word >> 16]
    return [c.astype(F32) * scales[2 * pair + r:2 * pair + r + 1, :] for r, c in enumerate(codes)]


def encode_kernel(state_ref, code_ref):
    powers = []
    for m in range(state_ref.shape[1] // 2):
        powers += store_pair(code_ref, m, [state_ref[0, 2 * m], state_ref[0, 2 * m + 1]])
    store_powers(code_ref, powers)


def decode_kernel(place_ref, code_ref, *refs):
    del place_ref
    state_ref = refs[-1]
    heads, rows = state_ref.shape[1:3]
    scales = load_scales(code_ref)
    for m in range(heads // 2):
        state_ref[0, 2 * m], state_ref[0, 2 * m + 1] = load_pair(code_ref, scales, m, rows)


def prepare_kernel(ids_ref, count_ref, q_ref, k_ref, g_ref, b_ref, t_ref, m_ref, aux_ref,
                   q_rows, k_rows, a_rows):
    live = count_ref[ids_ref[pl.program_id(0)]]
    length, value_heads = g_ref.shape[1:]
    key_heads = value_heads // 2
    q_rows[...] = q_ref[0].astype(F32)
    k_rows[...] = k_ref[0].astype(F32)
    tokens = lax.broadcasted_iota(jnp.int32, (length, value_heads), 0)
    g = jnp.where(tokens < live, g_ref[0].astype(F32), 0.0)
    b = jnp.where(tokens < live, b_ref[0].astype(F32), 0.0)
    row = lax.broadcasted_iota(jnp.int32, (length, length), 0)
    col = lax.broadcasted_iota(jnp.int32, (length, length), 1)
    inclusive = row >= col
    strict = row > col
    diagonal = row == col
    ones_low = inclusive.astype(F32).astype(BF16)
    ones_up = (row <= col).astype(F32).astype(BF16)
    g_narrow = g.astype(BF16)
    g_col = dot(ones_low, g_narrow)
    g_row = dot_tn(g_narrow, ones_up)
    lane = lax.broadcasted_iota(jnp.int32, (BASE, length), 1)
    sub = lax.broadcasted_iota(jnp.int32, (BASE, length), 0)
    parts = length // BASE
    unit_cols = []
    compact = []
    for m in range(key_heads):
        q = q_rows[pl.ds(m, length, stride=key_heads), :].astype(BF16)
        k = k_rows[pl.ds(m, length, stride=key_heads), :].astype(BF16)
        both = dot_nt(jnp.concatenate([k, q], axis=0), k)
        kk = both[:length]
        qk = both[length:]
        squares = jnp.where(diagonal, kk, 0.0)
        n_row = lax.rsqrt(jnp.sum(squares, axis=0, keepdims=True) + norm_epsilon)
        n_col = lax.rsqrt(jnp.sum(squares, axis=1, keepdims=True) + norm_epsilon)
        unit_cols += [n_col, n_col]
        kk = kk * n_row * n_col
        qk = qk * n_row
        for r in range(2):
            h = 2 * m + r
            decay = jnp.exp(jnp.where(inclusive, g_col[:, h:h + 1] - g_row[h:h + 1, :], 0.0))
            m_ref[0, h] = jnp.where(inclusive, qk * decay, 0.0)
            a = jnp.where(strict, kk * decay * b[:, h:h + 1], 0.0)
            a_rows[h] = a
            piece = jnp.zeros((BASE, length), F32)
            for p in range(parts):
                piece = jnp.where(lane // BASE == p, a[p * BASE:(p + 1) * BASE], piece)
            compact.append(piece)
    inverses = [(lane % BASE == sub).astype(F32) for _ in range(value_heads)]
    for j in range(BASE - 1):
        index = (lane // BASE) * BASE + j
        for h in range(value_heads):
            factor = jnp.take_along_axis(compact[h], index, axis=1)
            inverses[h] = inverses[h] - factor * inverses[h][j:j + 1, :]
    block_masks = [lane // BASE == p for p in range(parts)]
    levels = []
    size = BASE
    while size < length:
        levels.append((size, range(size, length, 2 * size)))
        size *= 2
    heads = range(value_heads)
    for h in heads:
        blocks = [jnp.where(block_masks[p], inverses[h], 0.0) for p in range(parts)]
        t_ref[0, h] = jnp.concatenate(blocks, axis=0)
    for size, starts in levels:
        columns = lax.broadcasted_iota(jnp.int32, (size, length), 1) // size
        empty = jnp.zeros((size, length), F32)
        steps = []
        for h in heads:
            lower = [
                jnp.where(columns == start // size - 1, a_rows[h, start:start + size, :], 0.0)
                for start in starts
            ]
            steps.append(dot3(jnp.concatenate(lower, axis=0), t_ref[0, h]))
        for h in heads:
            spread = []
            for n in range(len(starts)):
                spread += [empty, steps[h][n * size:(n + 1) * size]]
            odd = jnp.concatenate([t_ref[0, h, start:start + size, :] for start in starts], axis=0)
            odd = odd - dot3(odd, jnp.concatenate(spread, axis=0))
            for n, start in enumerate(starts):
                t_ref[0, h, start:start + size, :] = odd[n * size:(n + 1) * size]
    units = jnp.concatenate(unit_cols, axis=1)
    growth = jnp.exp(g_col)
    rest = jnp.exp(g_col[length - 1:length, :] - g_col) * units
    aux_ref[0] = jnp.concatenate([growth, b, b * growth * units, rest], axis=1)


def advance_kernel(coded, ids_ref, parents_ref, count_ref, place_ref, q_ref, k_ref, v_ref, t_ref,
                   m_ref, aux_ref, gain_ref, s_ref, *refs):
    del parents_ref, place_ref
    mixed_ref, state_ref, q_rows, k_rows, v_rows, o_rows = refs[-6:]
    number = ids_ref[pl.program_id(0)]
    live = count_ref[number]
    value_heads, length = t_ref.shape[1:3]
    key_heads = value_heads // 2
    width = s_ref.shape[-1]
    key_dim = k_ref.shape[-1]
    scales = load_scales(s_ref)
    powers = []
    q_rows[...] = q_ref[0].astype(F32)
    k_rows[...] = k_ref[0].astype(F32)
    v_rows[...] = v_ref[0].astype(F32)
    aux = aux_ref[0]
    gain = gain_ref[...].astype(F32)
    alive = lax.broadcasted_iota(jnp.int32, (length, width), 0) < live
    columns = lambda n, h: aux[:, n * value_heads + h:n * value_heads + h + 1]
    half = lambda pair, r: pair[:, r * width:(r + 1) * width]
    key_parts, applied = [], []
    for m in range(key_heads):
        q = q_rows[pl.ds(m, length, stride=key_heads), :].astype(BF16)
        k = k_rows[pl.ds(m, length, stride=key_heads), :].astype(BF16)
        s_high, s_low = split(jnp.concatenate(load_pair(s_ref, scales, m, key_dim), axis=1))
        kq = jnp.concatenate([k, q], axis=0)
        key_parts.append(k)
        applied.append(
            dot(jnp.concatenate([kq, kq], axis=1), jnp.concatenate([s_high, s_low], axis=0))
        )
    fixed = []
    for h in range(value_heads):
        v = v_rows[pl.ds(h, length, stride=value_heads), :]
        right = columns(1, h) * v - columns(2, h) * half(applied[h // 2][:length], h % 2)
        fixed.append(dot3(t_ref[0, h], right))
    for m in range(key_heads):
        k = key_parts[m]
        update = jnp.concatenate([columns(3, 2 * m + r) * fixed[2 * m + r] for r in range(2)], axis=1)
        u_high, u_low = split(update)
        added = dot_tn(jnp.concatenate([k, k], axis=0), jnp.concatenate([u_high, u_low], axis=0))
        states = load_pair(s_ref, scales, m, key_dim)
        later = []
        for r in range(2):
            last = aux[length - 1:length, 2 * m + r:2 * m + r + 1]
            later.append(last * states[r] + half(added, r))
        if coded:
            powers += store_pair(state_ref, m, later)
        else:
            state_ref[0, 2 * m], state_ref[0, 2 * m + 1] = later
    for h in range(value_heads):
        out = columns(0, h) * half(applied[h // 2][length:], h % 2) + dot3(m_ref[0, h], fixed[h])
        mean_square = jnp.mean(out * out, axis=1, keepdims=True)
        normed = out * lax.rsqrt(mean_square + norm_epsilon) * gain
        o_rows[pl.ds(h, length, stride=value_heads), :] = jnp.where(alive, normed, 0.0)
    if coded:
        store_powers(state_ref, powers)
    mixed_ref[0] = o_rows[...].astype(BF16)


def prepare(ids, counts, queries, keys, decay, rate):
    expansions = ids.shape[0]
    length, value_heads = decay.shape[1:]
    rows, key_dim = queries.shape[1:]
    square = (expansions, value_heads, length, length)
    own = lambda shape: pl.BlockSpec((1,) + shape, lambda i, ids, c: (ids[i],) + (0,) * len(shape))
    block = lambda shape: pl.BlockSpec((1,) + shape, lambda i, ids, c: (i,) + (0,) * len(shape))
    work = expansions * value_heads
    return pl.pallas_call(
        prepare_kernel,
        out_shape=(
            jax.ShapeDtypeStruct(square, F32),
            jax.ShapeDtypeStruct(square, F32),
            jax.ShapeDtypeStruct((expansions, length, 4 * value_heads), F32),
        ),
        grid_spec=pltpu.PrefetchScalarGridSpec(
            num_scalar_prefetch=2,
            grid=(expansions,),
            in_specs=[
                own((rows, key_dim)),
                own((rows, key_dim)),
                own((length, value_heads)),
                own((length, value_heads)),
            ],
            out_specs=(
                block(square[1:]),
                block(square[1:]),
                block((length, 4 * value_heads)),
            ),
            scratch_shapes=[
                pltpu.VMEM((rows, key_dim), F32),
                pltpu.VMEM((rows, key_dim), F32),
                pltpu.VMEM((value_heads, length, length), F32),
            ],
        ),
        compiler_params=pltpu.CompilerParams(vmem_limit_bytes=VMEM_BYTES),
        cost_estimate=pl.CostEstimate(
            flops=work * 30 * 2 * length**3,
            bytes_accessed=work * 2 * 4 * length * length,
            transcendentals=work * length * length,
        ),
        name="prepare",
    )(ids, counts, queries, keys, decay, rate)


def encode(states):
    count, heads, key_dim, width = states.shape
    rows = heads // 2 * key_dim + CODE_ROWS
    return pl.pallas_call(
        encode_kernel,
        out_shape=jax.ShapeDtypeStruct((count, rows, width), jnp.int32),
        grid=(count,),
        in_specs=[pl.BlockSpec((1, heads, key_dim, width), lambda i: (i, 0, 0, 0))],
        out_specs=pl.BlockSpec((1, rows, width), lambda i: (i, 0, 0)),
        compiler_params=pltpu.CompilerParams(vmem_limit_bytes=VMEM_BYTES),
        name="encode",
    )(states)


def decode(place, codes, final):
    count, rows, width = codes.shape
    heads, key_dim = final.shape[1:3]
    return pl.pallas_call(
        decode_kernel,
        out_shape=jax.ShapeDtypeStruct(final.shape, final.dtype),
        grid_spec=pltpu.PrefetchScalarGridSpec(
            num_scalar_prefetch=1,
            grid=(count,),
            in_specs=[
                pl.BlockSpec((1, rows, width), lambda i, place: (i, 0, 0)),
                pl.BlockSpec(memory_space=pl.ANY),
            ],
            out_specs=pl.BlockSpec(
                (1, heads, key_dim, width), lambda i, place: (place[0] + i, 0, 0, 0)
            ),
        ),
        input_output_aliases={2: 0},
        compiler_params=pltpu.CompilerParams(vmem_limit_bytes=VMEM_BYTES),
        name="decode",
    )(place, codes, final)


def advance(ids, parents, counts, place, first, queries, keys, values, inverse, mixing, aux, gain,
            states, mixed, coded):
    steps = ids.shape[0]
    expansions = queries.shape[0]
    value_heads, length = inverse.shape[1:3]
    rows, key_dim = queries.shape[1:]
    width = values.shape[-1]
    state_rows = states.shape[1]
    own = lambda shape: pl.BlockSpec(
        (1,) + shape, lambda i, ids, par, c, p: (ids[i],) + (0,) * len(shape)
    )
    step = lambda shape: pl.BlockSpec(
        (1,) + shape, lambda i, ids, par, c, p: (first + i,) + (0,) * len(shape)
    )
    if coded:
        state_shape = jax.ShapeDtypeStruct((steps, state_rows, width), jnp.int32)
        state_spec = pl.BlockSpec((1, state_rows, width), lambda i, ids, par, c, p: (i, 0, 0))
    else:
        state_shape = jax.ShapeDtypeStruct((expansions, value_heads, key_dim, width), F32)
        state_spec = pl.BlockSpec(
            (1, value_heads, key_dim, width), lambda i, ids, par, c, p: (p[0] + i, 0, 0, 0)
        )
    in_specs = [
        own((rows, key_dim)),
        own((rows, key_dim)),
        own((length * value_heads, width)),
        step((value_heads, length, length)),
        step((value_heads, length, length)),
        step((length, 4 * value_heads)),
        pl.BlockSpec((1, width), lambda i, ids, par, c, p: (0, 0)),
        pl.BlockSpec((1, state_rows, width), lambda i, ids, par, c, p: (par[i], 0, 0)),
    ]
    operands = [ids, parents, counts, place, queries, keys, values, inverse, mixing, aux, gain, states]
    aliases = {}
    if mixed is not None:
        aliases = {len(operands): 0}
        operands.append(mixed)
        in_specs.append(pl.BlockSpec(memory_space=pl.ANY))
    work = steps * value_heads
    return pl.pallas_call(
        functools.partial(advance_kernel, coded),
        out_shape=(jax.ShapeDtypeStruct(values.shape, BF16), state_shape),
        grid_spec=pltpu.PrefetchScalarGridSpec(
            num_scalar_prefetch=4,
            grid=(steps,),
            in_specs=in_specs,
            out_specs=(own((length * value_heads, width)), state_spec),
            scratch_shapes=[
                pltpu.VMEM((rows, key_dim), F32),
                pltpu.VMEM((rows, key_dim), F32),
                pltpu.VMEM((length * value_heads, width), F32),
                pltpu.VMEM((length * value_heads, width), F32),
            ],
        ),
        input_output_aliases=aliases,
        compiler_params=pltpu.CompilerParams(vmem_limit_bytes=VMEM_BYTES),
        cost_estimate=pl.CostEstimate(
            flops=work * 12 * 2 * length**3,
            bytes_accessed=work * 5 * 4 * length * length,
            transcendentals=work * length,
        ),
        name="advance",
    )(*operands)


def shards(queries, keys, values, log_decay, write_rate, norm_gain, parent_cache, order,
           parent_owner, parent_slot, token_count):
    seq_count = lax.axis_size("seq")
    me = lax.axis_index("seq")
    expansions, length, key_heads, key_dim = queries.shape
    value_heads = 2 * key_heads
    width = values.shape[-1]
    per_peer = expansions // seq_count
    cache_rows = parent_cache.shape[0]
    codes = encode(parent_cache.reshape(cache_rows, value_heads, key_dim, width))
    states = lax.all_gather(codes, "seq", axis=0, tiled=True)
    start = me * expansions
    own = lambda table: lax.dynamic_slice_in_dim(table, start, expansions)
    counts = own(token_count)
    parents = own(parent_owner) * cache_rows + own(parent_slot)
    sends = lax.dynamic_slice_in_dim(
        order.reshape(seq_count, expansions), me * per_peer, per_peer, 1
    ) - start
    shifts = sorted(range(seq_count), key=lambda s: -min(s, seq_count - s))
    targets = lax.rem(me + jnp.array(shifts, jnp.int32), seq_count)
    ids = jnp.take(sends, targets, axis=0).reshape(-1)
    parents = jnp.take(parents, ids)
    remote = expansions - per_peer
    q = queries.reshape(expansions, length * key_heads, key_dim)
    k = keys.reshape(expansions, length * key_heads, key_dim)
    v = values.reshape(expansions, length * value_heads, width)
    decay = log_decay.reshape(expansions, length, value_heads)
    rate = write_rate.reshape(expansions, length, value_heads)
    gain = norm_gain.reshape(1, width)
    pieces = prepare(ids[:remote], counts, q, k, decay, rate)
    mixed = None
    arriving = []
    for at, shift in enumerate(shifts):
        first = at * per_peer
        if not shift:
            late, _ = lax.optimization_barrier((ids[remote:], codes))
            pieces = prepare(late, counts, q, k, decay, rate)
            first = 0
        here = slice(at * per_peer, (at + 1) * per_peer)
        place = (lax.rem(me + seq_count - shift, seq_count) * per_peer).reshape(1)
        mixed, codes = advance(ids[here], parents[here], counts, place, first, q, k, v, *pieces,
                               gain, states, mixed, bool(shift))
        if shift:
            pairs = [(d, (d + shift) % seq_count) for d in range(seq_count)]
            arriving.append((place, lax.ppermute(codes, "seq", pairs)))
    final = codes
    for place, codes in arriving:
        final = decode(place, codes, final)
    return (
        mixed.reshape(values.shape),
        final.reshape((expansions,) + parent_cache.shape[1:]),
    )


def solution(mesh):
    heads = ("head", "sub")
    rows = ("groups", "seq")
    placed = (
        P(rows, None, heads, None),
        P(rows, None, heads, None),
        P(rows, None, heads, None, None),
        P(rows, None, heads, None),
        P(rows, None, heads, None),
        P(),
        P(rows, heads, None, None, None),
        P("groups"),
        P("groups"),
        P("groups"),
        P("groups"),
    )
    return jax.shard_map(
        shards,
        mesh=mesh,
        in_specs=placed,
        out_specs=(P(rows, None, heads, None, None), P(rows, heads, None, None, None)),
        check_vma=False,
    )
```

```python
import functools

import jax
import jax.numpy as jnp
from jax import lax
from jax.experimental import pallas as pl
from jax.experimental.pallas import tpu as pltpu
from jax.sharding import PartitionSpec as P

norm_epsilon = 1e-06
BASE = 16
F32 = jnp.float32
BF16 = jnp.bfloat16
VMEM_BYTES = 56 * 1024 * 1024


def split(x):
    high = x.astype(BF16)
    low = (x - high.astype(F32)).astype(BF16)
    return high, low


def dot(a, b):
    return jnp.dot(a, b, preferred_element_type=F32)


def dot_nt(a, b):
    return lax.dot_general(a, b, (((1,), (1,)), ((), ())), preferred_element_type=F32)


def dot_tn(a, b):
    return lax.dot_general(a, b, (((0,), (0,)), ((), ())), preferred_element_type=F32)


def dot3(a, b):
    a_high, a_low = split(a)
    b_high, b_low = split(b)
    right = jnp.concatenate([b_high, b_low], axis=1)
    both = dot(jnp.concatenate([a_high, a_low], axis=1), jnp.concatenate([right, right], axis=0))
    width = b.shape[1]
    return both[:, :width] + both[:, width:]


CODE_BITS = 15
CODE_ROWS = 8


def code_state(state):
    largest = jnp.maximum(jnp.max(jnp.abs(state), axis=0, keepdims=True), 1e-30)
    power = jnp.ceil(jnp.log2(largest)) - CODE_BITS
    limit = float(2**CODE_BITS - 1)
    code = jnp.clip(jnp.round(state * jnp.exp2(-power)), -limit, limit)
    return code.astype(jnp.int32), power.astype(jnp.int32)


def store_pair(code_ref, pair, states):
    (low, low_power), (high, high_power) = [code_state(state) for state in states]
    rows = low.shape[0]
    code_ref[0, pair * rows:(pair + 1) * rows, :] = (high << 16) | (low & 0xFFFF)
    return [low_power, high_power]


def store_powers(code_ref, powers):
    rows = code_ref.shape[1] - CODE_ROWS
    spare = [jnp.zeros_like(powers[0])] * (CODE_ROWS - len(powers))
    code_ref[0, rows:, :] = jnp.concatenate(powers + spare, axis=0)


def load_scales(code_ref):
    rows = code_ref.shape[1] - CODE_ROWS
    return jnp.exp2(code_ref[0, rows:, :].astype(F32))


def load_pair(code_ref, scales, pair, rows):
    word = code_ref[0, pair * rows:(pair + 1) * rows, :]
    codes = [(word << 16) >> 16, word >> 16]
    return [c.astype(F32) * scales[2 * pair + r:2 * pair + r + 1, :] for r, c in enumerate(codes)]


def encode_kernel(state_ref, code_ref):
    powers = []
    for m in range(state_ref.shape[1] // 2):
        powers += store_pair(code_ref, m, [state_ref[0, 2 * m], state_ref[0, 2 * m + 1]])
    store_powers(code_ref, powers)


def decode_kernel(chunks, steps, place_ref, *refs):
    del place_ref
    state_ref = refs[-1]
    heads, rows = state_ref.shape[1:3]
    for c in range(chunks):
        @pl.when(lax.div(pl.program_id(0), steps) == c)
        def _(code_ref=refs[c]):
            scales = load_scales(code_ref)
            for m in range(heads // 2):
                state_ref[0, 2 * m], state_ref[0, 2 * m + 1] = load_pair(code_ref, scales, m, rows)


def prepare_kernel(ids_ref, count_ref, q_ref, k_ref, g_ref, b_ref, t_ref, m_ref, aux_ref,
                   q_rows, k_rows, a_rows):
    live = count_ref[ids_ref[pl.program_id(0)]]
    length, value_heads = g_ref.shape[1:]
    key_heads = value_heads // 2
    q_rows[...] = q_ref[0].astype(F32)
    k_rows[...] = k_ref[0].astype(F32)
    tokens = lax.broadcasted_iota(jnp.int32, (length, value_heads), 0)
    g = jnp.where(tokens < live, g_ref[0].astype(F32), 0.0)
    b = jnp.where(tokens < live, b_ref[0].astype(F32), 0.0)
    row = lax.broadcasted_iota(jnp.int32, (length, length), 0)
    col = lax.broadcasted_iota(jnp.int32, (length, length), 1)
    inclusive = row >= col
    strict = row > col
    diagonal = row == col
    ones_low = inclusive.astype(F32).astype(BF16)
    ones_up = (row <= col).astype(F32).astype(BF16)
    g_narrow = g.astype(BF16)
    g_col = dot(ones_low, g_narrow)
    g_row = dot_tn(g_narrow, ones_up)
    lane = lax.broadcasted_iota(jnp.int32, (BASE, length), 1)
    sub = lax.broadcasted_iota(jnp.int32, (BASE, length), 0)
    parts = length // BASE
    unit_cols = []
    compact = []
    for m in range(key_heads):
        q = q_rows[pl.ds(m, length, stride=key_heads), :].astype(BF16)
        k = k_rows[pl.ds(m, length, stride=key_heads), :].astype(BF16)
        both = dot_nt(jnp.concatenate([k, q], axis=0), k)
        kk = both[:length]
        qk = both[length:]
        squares = jnp.where(diagonal, kk, 0.0)
        n_row = lax.rsqrt(jnp.sum(squares, axis=0, keepdims=True) + norm_epsilon)
        n_col = lax.rsqrt(jnp.sum(squares, axis=1, keepdims=True) + norm_epsilon)
        unit_cols += [n_col, n_col]
        kk = kk * n_row * n_col
        qk = qk * n_row
        for r in range(2):
            h = 2 * m + r
            decay = jnp.exp(jnp.where(inclusive, g_col[:, h:h + 1] - g_row[h:h + 1, :], 0.0))
            m_ref[0, h] = jnp.where(inclusive, qk * decay, 0.0)
            a = jnp.where(strict, kk * decay * b[:, h:h + 1], 0.0)
            a_rows[h] = a
            piece = jnp.zeros((BASE, length), F32)
            for p in range(parts):
                piece = jnp.where(lane // BASE == p, a[p * BASE:(p + 1) * BASE], piece)
            compact.append(piece)
    inverses = [(lane % BASE == sub).astype(F32) for _ in range(value_heads)]
    for j in range(BASE - 1):
        index = (lane // BASE) * BASE + j
        for h in range(value_heads):
            factor = jnp.take_along_axis(compact[h], index, axis=1)
            inverses[h] = inverses[h] - factor * inverses[h][j:j + 1, :]
    block_masks = [lane // BASE == p for p in range(parts)]
    levels = []
    size = BASE
    while size < length:
        levels.append((size, range(size, length, 2 * size)))
        size *= 2
    heads = range(value_heads)
    for h in heads:
        blocks = [jnp.where(block_masks[p], inverses[h], 0.0) for p in range(parts)]
        t_ref[0, h] = jnp.concatenate(blocks, axis=0)
    for size, starts in levels:
        columns = lax.broadcasted_iota(jnp.int32, (size, length), 1) // size
        empty = jnp.zeros((size, length), F32)
        steps = []
        for h in heads:
            lower = [
                jnp.where(columns == start // size - 1, a_rows[h, start:start + size, :], 0.0)
                for start in starts
            ]
            steps.append(dot3(jnp.concatenate(lower, axis=0), t_ref[0, h]))
        for h in heads:
            spread = []
            for n in range(len(starts)):
                spread += [empty, steps[h][n * size:(n + 1) * size]]
            odd = jnp.concatenate([t_ref[0, h, start:start + size, :] for start in starts], axis=0)
            odd = odd - dot3(odd, jnp.concatenate(spread, axis=0))
            for n, start in enumerate(starts):
                t_ref[0, h, start:start + size, :] = odd[n * size:(n + 1) * size]
    units = jnp.concatenate(unit_cols, axis=1)
    growth = jnp.exp(g_col)
    rest = jnp.exp(g_col[length - 1:length, :] - g_col) * units
    aux_ref[0] = jnp.concatenate([growth, b, b * growth * units, rest], axis=1)


def advance_kernel(coded, ids_ref, parents_ref, count_ref, place_ref, q_ref, k_ref, v_ref, t_ref,
                   m_ref, aux_ref, gain_ref, s_ref, *refs):
    del parents_ref, place_ref
    mixed_ref, state_ref, q_rows, k_rows, v_rows, o_rows = refs[-6:]
    number = ids_ref[pl.program_id(0)]
    live = count_ref[number]
    value_heads, length = t_ref.shape[1:3]
    key_heads = value_heads // 2
    width = s_ref.shape[-1]
    key_dim = k_ref.shape[-1]
    scales = load_scales(s_ref)
    powers = []
    q_rows[...] = q_ref[0].astype(F32)
    k_rows[...] = k_ref[0].astype(F32)
    v_rows[...] = v_ref[0].astype(F32)
    aux = aux_ref[0]
    gain = gain_ref[...].astype(F32)
    alive = lax.broadcasted_iota(jnp.int32, (length, width), 0) < live
    columns = lambda n, h: aux[:, n * value_heads + h:n * value_heads + h + 1]
    half = lambda pair, r: pair[:, r * width:(r + 1) * width]
    key_parts, applied = [], []
    for m in range(key_heads):
        q = q_rows[pl.ds(m, length, stride=key_heads), :].astype(BF16)
        k = k_rows[pl.ds(m, length, stride=key_heads), :].astype(BF16)
        s_high, s_low = split(jnp.concatenate(load_pair(s_ref, scales, m, key_dim), axis=1))
        kq = jnp.concatenate([k, q], axis=0)
        key_parts.append(k)
        applied.append(
            dot(jnp.concatenate([kq, kq], axis=1), jnp.concatenate([s_high, s_low], axis=0))
        )
    fixed = []
    for h in range(value_heads):
        v = v_rows[pl.ds(h, length, stride=value_heads), :]
        right = columns(1, h) * v - columns(2, h) * half(applied[h // 2][:length], h % 2)
        fixed.append(dot3(t_ref[0, h], right))
    for m in range(key_heads):
        k = key_parts[m]
        update = jnp.concatenate([columns(3, 2 * m + r) * fixed[2 * m + r] for r in range(2)], axis=1)
        u_high, u_low = split(update)
        added = dot_tn(jnp.concatenate([k, k], axis=0), jnp.concatenate([u_high, u_low], axis=0))
        states = load_pair(s_ref, scales, m, key_dim)
        later = []
        for r in range(2):
            last = aux[length - 1:length, 2 * m + r:2 * m + r + 1]
            later.append(last * states[r] + half(added, r))
        if coded:
            powers += store_pair(state_ref, m, later)
        else:
            state_ref[0, 2 * m], state_ref[0, 2 * m + 1] = later
    for h in range(value_heads):
        out = columns(0, h) * half(applied[h // 2][length:], h % 2) + dot3(m_ref[0, h], fixed[h])
        mean_square = jnp.mean(out * out, axis=1, keepdims=True)
        normed = out * lax.rsqrt(mean_square + norm_epsilon) * gain
        o_rows[pl.ds(h, length, stride=value_heads), :] = jnp.where(alive, normed, 0.0)
    if coded:
        store_powers(state_ref, powers)
    mixed_ref[0] = o_rows[...].astype(BF16)


def prepare(ids, counts, queries, keys, decay, rate):
    expansions = ids.shape[0]
    length, value_heads = decay.shape[1:]
    rows, key_dim = queries.shape[1:]
    square = (expansions, value_heads, length, length)
    own = lambda shape: pl.BlockSpec((1,) + shape, lambda i, ids, c: (ids[i],) + (0,) * len(shape))
    block = lambda shape: pl.BlockSpec((1,) + shape, lambda i, ids, c: (i,) + (0,) * len(shape))
    work = expansions * value_heads
    return pl.pallas_call(
        prepare_kernel,
        out_shape=(
            jax.ShapeDtypeStruct(square, F32),
            jax.ShapeDtypeStruct(square, F32),
            jax.ShapeDtypeStruct((expansions, length, 4 * value_heads), F32),
        ),
        grid_spec=pltpu.PrefetchScalarGridSpec(
            num_scalar_prefetch=2,
            grid=(expansions,),
            in_specs=[
                own((rows, key_dim)),
                own((rows, key_dim)),
                own((length, value_heads)),
                own((length, value_heads)),
            ],
            out_specs=(
                block(square[1:]),
                block(square[1:]),
                block((length, 4 * value_heads)),
            ),
            scratch_shapes=[
                pltpu.VMEM((rows, key_dim), F32),
                pltpu.VMEM((rows, key_dim), F32),
                pltpu.VMEM((value_heads, length, length), F32),
            ],
        ),
        compiler_params=pltpu.CompilerParams(vmem_limit_bytes=VMEM_BYTES),
        cost_estimate=pl.CostEstimate(
            flops=work * 2 * length**2,
            bytes_accessed=work * length,
            transcendentals=work,
        ),
        name="prepare",
    )(ids, counts, queries, keys, decay, rate)


def encode(states):
    count, heads, key_dim, width = states.shape
    rows = heads // 2 * key_dim + CODE_ROWS
    return pl.pallas_call(
        encode_kernel,
        out_shape=jax.ShapeDtypeStruct((count, rows, width), jnp.int32),
        grid=(count,),
        in_specs=[pl.BlockSpec((1, heads, key_dim, width), lambda i: (i, 0, 0, 0))],
        out_specs=pl.BlockSpec((1, rows, width), lambda i: (i, 0, 0)),
        compiler_params=pltpu.CompilerParams(vmem_limit_bytes=VMEM_BYTES),
        name="encode",
    )(states)


def decode(places, codes, final):
    chunks = len(codes)
    count, rows, width = codes[0].shape
    heads, key_dim = final.shape[1:3]
    chunk = lambda c: pl.BlockSpec(
        (1, rows, width),
        lambda i, place: (jnp.minimum(jnp.maximum(i - c * count, 0), count - 1), 0, 0),
    )
    return pl.pallas_call(
        functools.partial(decode_kernel, chunks, count),
        out_shape=jax.ShapeDtypeStruct(final.shape, final.dtype),
        grid_spec=pltpu.PrefetchScalarGridSpec(
            num_scalar_prefetch=1,
            grid=(chunks * count,),
            in_specs=[chunk(c) for c in range(chunks)] + [pl.BlockSpec(memory_space=pl.ANY)],
            out_specs=pl.BlockSpec(
                (1, heads, key_dim, width),
                lambda i, place: (place[lax.div(i, count)] + lax.rem(i, count), 0, 0, 0),
            ),
        ),
        input_output_aliases={1 + chunks: 0},
        compiler_params=pltpu.CompilerParams(vmem_limit_bytes=VMEM_BYTES),
        name="decode",
    )(places, *codes, final)


def advance(ids, parents, counts, place, first, queries, keys, values, inverse, mixing, aux, gain,
            states, mixed, coded):
    steps = ids.shape[0]
    expansions = queries.shape[0]
    value_heads, length = inverse.shape[1:3]
    rows, key_dim = queries.shape[1:]
    width = values.shape[-1]
    state_rows = states.shape[1]
    own = lambda shape: pl.BlockSpec(
        (1,) + shape, lambda i, ids, par, c, p: (ids[i],) + (0,) * len(shape)
    )
    step = lambda shape: pl.BlockSpec(
        (1,) + shape, lambda i, ids, par, c, p: (first + i,) + (0,) * len(shape)
    )
    if coded:
        state_shape = jax.ShapeDtypeStruct((steps, state_rows, width), jnp.int32)
        state_spec = pl.BlockSpec((1, state_rows, width), lambda i, ids, par, c, p: (i, 0, 0))
    else:
        state_shape = jax.ShapeDtypeStruct((expansions, value_heads, key_dim, width), F32)
        state_spec = pl.BlockSpec(
            (1, value_heads, key_dim, width), lambda i, ids, par, c, p: (p[0] + i, 0, 0, 0)
        )
    in_specs = [
        own((rows, key_dim)),
        own((rows, key_dim)),
        own((length * value_heads, width)),
        step((value_heads, length, length)),
        step((value_heads, length, length)),
        step((length, 4 * value_heads)),
        pl.BlockSpec((1, width), lambda i, ids, par, c, p: (0, 0)),
        pl.BlockSpec((1, state_rows, width), lambda i, ids, par, c, p: (par[i], 0, 0)),
    ]
    operands = [ids, parents, counts, place, queries, keys, values, inverse, mixing, aux, gain, states]
    aliases = {}
    if mixed is not None:
        aliases = {len(operands): 0}
        operands.append(mixed)
        in_specs.append(pl.BlockSpec(memory_space=pl.ANY))
    work = steps * value_heads
    return pl.pallas_call(
        functools.partial(advance_kernel, coded),
        out_shape=(jax.ShapeDtypeStruct(values.shape, BF16), state_shape),
        grid_spec=pltpu.PrefetchScalarGridSpec(
            num_scalar_prefetch=4,
            grid=(steps,),
            in_specs=in_specs,
            out_specs=(own((length * value_heads, width)), state_spec),
            scratch_shapes=[
                pltpu.VMEM((rows, key_dim), F32),
                pltpu.VMEM((rows, key_dim), F32),
                pltpu.VMEM((length * value_heads, width), F32),
                pltpu.VMEM((length * value_heads, width), F32),
            ],
        ),
        input_output_aliases=aliases,
        compiler_params=pltpu.CompilerParams(vmem_limit_bytes=VMEM_BYTES),
        cost_estimate=pl.CostEstimate(
            flops=work * 2 * length**2,
            bytes_accessed=work * length,
            transcendentals=work,
        ),
        name="advance",
    )(*operands)


def shards(queries, keys, values, log_decay, write_rate, norm_gain, parent_cache, order,
           parent_owner, parent_slot, token_count):
    seq_count = lax.axis_size("seq")
    me = lax.axis_index("seq")
    expansions, length, key_heads, key_dim = queries.shape
    value_heads = 2 * key_heads
    width = values.shape[-1]
    per_peer = expansions // seq_count
    cache_rows = parent_cache.shape[0]
    codes = encode(parent_cache.reshape(cache_rows, value_heads, key_dim, width))
    states = lax.all_gather(codes, "seq", axis=0, tiled=True)
    start = me * expansions
    own = lambda table: lax.dynamic_slice_in_dim(table, start, expansions)
    counts = own(token_count)
    parents = own(parent_owner) * cache_rows + own(parent_slot)
    sends = lax.dynamic_slice_in_dim(
        order.reshape(seq_count, expansions), me * per_peer, per_peer, 1
    ) - start
    shifts = sorted(range(seq_count), key=lambda s: -min(s, seq_count - s))
    targets = lax.rem(me + jnp.array(shifts, jnp.int32), seq_count)
    ids = jnp.take(sends, targets, axis=0).reshape(-1)
    parents = jnp.take(parents, ids)
    remote = expansions - per_peer
    q = queries.reshape(expansions, length * key_heads, key_dim)
    k = keys.reshape(expansions, length * key_heads, key_dim)
    v = values.reshape(expansions, length * value_heads, width)
    decay = log_decay.reshape(expansions, length, value_heads)
    rate = write_rate.reshape(expansions, length, value_heads)
    gain = norm_gain.reshape(1, width)
    pieces = prepare(ids[:remote], counts, q, k, decay, rate)
    mixed = None
    arriving = []
    for at, shift in enumerate(shifts):
        first = at * per_peer
        if not shift:
            late, _ = lax.optimization_barrier((ids[remote:], codes))
            pieces = prepare(late, counts, q, k, decay, rate)
            first = 0
        here = slice(at * per_peer, (at + 1) * per_peer)
        place = (lax.rem(me + seq_count - shift, seq_count) * per_peer).reshape(1)
        mixed, codes = advance(ids[here], parents[here], counts, place, first, q, k, v, *pieces,
                               gain, states, mixed, bool(shift))
        if shift:
            pairs = [(d, (d + shift) % seq_count) for d in range(seq_count)]
            arriving.append((place, lax.ppermute(codes, "seq", pairs)))
    final = codes
    for group in (arriving[:1], arriving[1:]):
        if group:
            places, codes = zip(*group)
            final = decode(jnp.concatenate(places), codes, final)
    return (
        mixed.reshape(values.shape),
        final.reshape((expansions,) + parent_cache.shape[1:]),
    )


def solution(mesh):
    heads = ("head", "sub")
    rows = ("groups", "seq")
    placed = (
        P(rows, None, heads, None),
        P(rows, None, heads, None),
        P(rows, None, heads, None, None),
        P(rows, None, heads, None),
        P(rows, None, heads, None),
        P(),
        P(rows, heads, None, None, None),
        P("groups"),
        P("groups"),
        P("groups"),
        P("groups"),
    )
    return jax.shard_map(
        shards,
        mesh=mesh,
        in_specs=placed,
        out_specs=(P(rows, None, heads, None, None), P(rows, heads, None, None, None)),
        check_vma=False,
    )
```
